256 devices in a mesh: dom: 64 (over z, y, core), grp: 4 (over x).
Axes of the slice: x: 4, y: 4, z: 8, core: 2. Of those that a mesh axis runs over, the one named last changes fastest.
Arguments:
- element_faces: int32 [4, 8192], P(None, 'dom'), may hold values from 0 to 8191, as said below
- interior_load: bfloat16 [80, 8192], P(None, 'dom'), may hold values from -6 to 6
- inverses: bfloat16 [80, 80, 8192], P('grp', None, 'dom'), may hold values from -0.625 to 0.625
- lift_operator: float32 [80, 240], P('grp'), may hold values from -0.625 to 0.625
- face_area: float32 [4, 8192], P(None, 'dom'), may hold values from 0.3 to 27
- columns: int32 [7, 8192], P(None, 'dom'), may hold values from -1 to 8191, as said below
- blocks: float32 [7, 60, 60, 8192], P(None, 'grp', None, 'dom'), may hold values from -0.00119 to 0.00119
- diagonal: float32 [60, 8192], P('grp', 'dom'), may hold values from 1.02 to 1.3
Outputs:
- solution: float32 [60, 8192], P('grp', 'dom')
- residual: float32 [60, 8192], P('grp', 'dom')
The draws below stay inside these ranges and needn't reach their ends.
Inputs may be any that keep to these rules, and one draw needn't show every extreme that they name: `element_faces`: every face block of an element is owned by the element's own index of dom or the one before or after it; an index owns the face blocks i * 128 to (i + 1) * 128 - 1. `columns`: slot 0 of a face block row holds the block itself. Every other nonnegative entry is a face block owned by the row's own index of dom or the one before or after it, and within one slot no number appears twice.
All inputs are finite; a program needn't handle non-finite values.
Results may differ from the reference program's by a relative error of at most 0.0003.
Values sent between devices are 32-bit elements; how exact they have to be, the bound alone decides.
A program may use at most 64 MiB of HBM per device.

```python
import jax
import jax.numpy as jnp
from jax import lax

FB = 60
NI = 80
SLOTS = 7
ITERS = 8
F_DEV = 128
E_DEV = 128
FACES = 8192
ELEMS = 8192
N_DOM = 64


def draw_columns(key, part):
    faces = F_DEV * N_DOM
    half = F_DEV // 2
    groups = faces // half
    position = jnp.arange(faces, dtype=jnp.int32)
    listing = [position]
    for slot_index in range(1, SLOTS):
        slot_key = jax.random.fold_in(key, slot_index + 11)
        shift_key, order_key, drop_key = jax.random.split(slot_key, 3)
        offset = jax.random.randint(shift_key, (), -half, half + 1, dtype=jnp.int32)
        target = position + offset
        inside = (target >= 0) & (target < faces)
        safe_target = jnp.clip(target, 0, faces - 1)
        scores = jax.random.randint(order_key, (groups, half), 0, 1 << 20, dtype=jnp.int32) * half + jnp.arange(half, dtype=jnp.int32)[None, :]
        shuffle = jnp.argsort(scores, axis=1).astype(jnp.int32)
        moved = safe_target // half * half + shuffle[safe_target // half, safe_target % half]
        kept = jax.random.randint(drop_key, (faces,), 0, 8, dtype=jnp.int32) > 0
        listing.append(jnp.where(inside & kept, moved, -1))
    return jnp.stack(listing).astype(jnp.int32)


def draw_element_faces(key, part):
    elements = E_DEV * N_DOM
    owner = jnp.arange(elements, dtype=jnp.int32) // E_DEV
    lowest = jnp.maximum(owner - 1, 0) * F_DEV
    highest = jnp.minimum(owner + 2, N_DOM) * F_DEV
    drawn = jax.random.randint(jax.random.fold_in(key, 5), (4, elements), lowest[None, :], highest[None, :], dtype=jnp.int32)
    return drawn.astype(jnp.int32)


def draw_face_area(key, part):
    elements = E_DEV * N_DOM
    ramp = 1.0 + 2.0 * jnp.arange(elements, dtype=jnp.float32) / elements
    exponent = jax.random.uniform(jax.random.fold_in(key, 7), (4, elements), jnp.float32, jnp.log(0.3), jnp.log(3.0))
    return (jnp.exp(exponent) * ramp[None, :]).astype(jnp.float32)


def draw_blocks(key, part):
    faces = F_DEV * N_DOM
    edge = 0.00119
    shape = (SLOTS, FB, FB, faces)
    block_key = jax.random.fold_in(key, 21)
    values = jax.random.uniform(block_key, shape, jnp.float32, -edge, edge)
    return values.astype(jnp.float32)


def levels(rng, extent, shards, smallest, largest):
    def one(dim, parts):
        steps = jax.random.uniform(jax.random.fold_in(jax.random.fold_in(rng, 6), dim), (parts,), jnp.float32, smallest / len(shards), largest / len(shards))
        return jnp.repeat(jnp.exp(steps), extent[dim] // parts).reshape((-1,) + (1,) * (len(extent) - dim - 1))

    factor_of = one(*shards[0])
    for cut in shards[1:]:
        factor_of = factor_of * one(*cut)
    return factor_of


def centred(stream_key, extent, width, bound, cuts=(), kind=jnp.bfloat16):
    factor_of = levels(stream_key, extent, cuts, -0.22, 0.18) if cuts else 1.0
    values = jax.random.normal(stream_key, extent, jnp.float32) * width * factor_of
    return jnp.minimum(jnp.maximum(values, -bound), bound).astype(kind)


def setup_inputs(seed: int = 0) -> dict:
    key_list = jax.random.split(jax.random.key(seed), 9)
    return {
        "element_faces": draw_element_faces(jax.random.fold_in(key_list[8], 71), 0),
        "interior_load": centred(key_list[1], (NI, ELEMS), 1.0, 6.0, ((1, 64),)),
        "inverses": centred(key_list[2], (NI, NI, ELEMS), NI ** -0.5, 0.625, ((0, 4), (2, 64))),
        "lift_operator": centred(key_list[3], (NI, 4 * FB), NI ** -0.5, 0.625, ((0, 4),), jnp.float32),
        "face_area": draw_face_area(jax.random.fold_in(key_list[8], 71), 0),
        "columns": draw_columns(jax.random.fold_in(key_list[8], 71), 0),
        "blocks": draw_blocks(jax.random.fold_in(key_list[8], 71), 0),
        "diagonal": jnp.clip(1.02 + 0.27999997 * jax.random.uniform(key_list[7], (FB, FACES), jnp.float32) ** levels(key_list[7], (FB, FACES), ((0, 4), (1, 64)), -0.2, 0.2), 1.02, 1.3),
    }


def operate(field, blocks, columns, diagonal):
    usable = columns >= 0
    index = jnp.where(usable, columns, 0).astype(jnp.int32)
    result = diagonal * field
    for slot_index in range(SLOTS):
        matrix = blocks[slot_index]
        picked = jnp.where(usable[slot_index][None, :], field[:, index[slot_index]], jnp.zeros((), field.dtype))
        result = result + jnp.einsum("ijf,jf->if", matrix, picked, precision=lax.Precision.HIGHEST)
        transposed = jnp.einsum("ijf,if->jf", matrix, field, precision=lax.Precision.HIGHEST)
        transposed = jnp.where(usable[slot_index][None, :], transposed, jnp.zeros((), field.dtype))
        result = result + jax.ops.segment_sum(transposed.T, index[slot_index], num_segments=FACES).T
    return result


def reference(element_faces, interior_load, inverses, lift_operator, face_area, columns, blocks, diagonal):
    interior = jnp.einsum("ije,je->ie", inverses.astype(jnp.float32), interior_load.astype(jnp.float32), precision=lax.Precision.HIGHEST)
    lifted = jnp.dot(lift_operator.T, interior, precision=lax.Precision.HIGHEST)
    contribution = -(lifted.reshape(4, FB, ELEMS) * face_area[:, None, :])
    entries = jnp.transpose(contribution, (0, 2, 1)).reshape(4 * ELEMS, FB)
    right_side = jax.ops.segment_sum(entries, element_faces.reshape(-1).astype(jnp.int32), num_segments=FACES).T
    solution = jnp.zeros_like(right_side)
    residual = right_side
    direction = right_side
    norm_now = jnp.sum(residual * residual)
    for iteration in range(ITERS):
        image = operate(direction, blocks, columns, diagonal)
        alpha = norm_now / jnp.sum(direction * image)
        solution = solution + alpha * direction
        residual = residual - alpha * image
        norm_next = jnp.sum(residual * residual)
        direction = residual + (norm_next / norm_now) * direction
        norm_now = norm_next
    return solution, residual
```

```python
import jax
import jax.numpy as jnp
from jax import lax
from jax.experimental import pallas as pl
from jax.experimental.pallas import tpu as pltpu
from jax.sharding import PartitionSpec as P

MESH = pl.DeviceIdType.MESH
F32 = jnp.float32
SHIFT = 1.16
FAR_FIRST = (2, 1, 3, 0)
LINKS = [(s, h) for h in FAR_FIRST for s in (1, -1)] + [(0, 2), (0, 1), (0, 3)]


def wide(row, rows):
    return jnp.broadcast_to(row, (rows, row.shape[-1]))


def pick(value, lanes):
    return jnp.take_along_axis(value, lanes, axis=1, mode="promise_in_bounds")


def kernel(
    n_dom, n_grp, faces_all,
    faces_h, load_h, inv_h, lift_h, area_h, cols_h, raw_h, diag_h,
    sol_ref, res_ref,
    faces, load, inv, lift, area, cols, raw, diag,
    blk, dg, lanes_of, part_of, back, slab, vrecv, tsend, trecv, ra, rb, st, cs,
    in_sem, vs_sem, vr_sem, ts_sem, tr_sem, as_sem, ar_sem, bs_sem, br_sem,
):
    d, g = lax.axis_index("dom"), lax.axis_index("grp")
    core = lax.rem(d, 2)
    y = lax.rem(d // 2, 4)
    z = d // 8
    zs = n_dom // 8
    slots = blk.shape[0]

    loads = [
        pltpu.make_async_copy(a, b, in_sem.at[i])
        for i, (a, b) in enumerate(
            [(inv_h, inv), (load_h, load), (lift_h, lift), (area_h, area), (faces_h, faces),
             (cols_h, cols), (diag_h, diag), (raw_h, raw)]
        )
    ]
    for c in loads:
        c.start()

    def link(s, h):
        return lax.rem(d + s + n_dom, n_dom), lax.rem(g + h, n_grp)

    def peer_a(dy, dx):
        y2 = lax.rem(y + dy, 4)
        return (z * 4 + y2) * 2 + core, lax.rem(g + dx, 4)

    def peer_b(dz, dc):
        z2 = lax.rem(z + dz, zs)
        return (z2 * 4 + y) * 2 + lax.rem(core + dc, 2), g

    group_a = [(a, b) for a in range(4) for b in range(4) if (a, b) != (0, 0)]
    group_b = [(a, b) for a in range(zs) for b in range(2) if (a, b) != (0, 0)]

    bar = pltpu.get_barrier_semaphore()
    greeted = (
        [link(s, h) for s, h in LINKS]
        + [peer_a(a, b) for a, b in group_a if a != 0]
        + [peer_b(a, b) for a, b in group_b]
    )
    for who in greeted:
        pl.semaphore_signal(bar, inc=1, device_id=who, device_id_type=MESH)

    def t_copy(par, s, h):
        peer = link(s, h)
        return pltpu.make_async_remote_copy(
            tsend.at[s + 1, peer[1]], trecv.at[par, s + 1, g], ts_sem.at[s + 1, h],
            tr_sem.at[par, s + 1, g], device_id=peer, device_id_type=MESH)

    def t_from(par, s, h):
        src = lax.rem(g + n_grp - h, n_grp)
        return pltpu.make_async_remote_copy(
            tsend.at[s + 1, g], trecv.at[par, s + 1, src], ts_sem.at[s + 1, h],
            tr_sem.at[par, s + 1, src], device_id=link(s, h), device_id_type=MESH)

    def v_copy(par, s, h):
        return pltpu.make_async_remote_copy(
            vrecv.at[par, 1, g], vrecv.at[par, 1 - s, g], vs_sem.at[s + 1, h],
            vr_sem.at[par, 1 - s, g], device_id=link(s, h), device_id_type=MESH)

    def v_from(par, s, h):
        src = lax.rem(g + n_grp - h, n_grp)
        return pltpu.make_async_remote_copy(
            vrecv.at[par, 1, g], vrecv.at[par, 1 - s, src], vs_sem.at[s + 1, h],
            vr_sem.at[par, 1 - s, src], device_id=link(s, h), device_id_type=MESH)

    def deliver_start(par):
        trecv[par, 1, g] = tsend[1, g]
        for s, h in LINKS:
            t_copy(par, s, h).start()

    def deliver_end(par):
        for s, h in LINKS:
            t_from(par, s, h).wait_recv()
        total = trecv[par, 0, 0]
        for s in range(3):
            for k in range(4):
                if (s, k) != (0, 0):
                    total = total + trecv[par, s, k]
        for s, h in LINKS:
            t_copy(par, s, h).wait_send()
        return total

    for c in loads[:5]:
        c.wait()
    interior = jnp.sum(inv[...].astype(F32) * load[...].astype(F32)[None], axis=1)
    base = (d - 1) * 128
    ends = lax.broadcasted_iota(jnp.int32, (384, 128), 0)
    out = jnp.zeros((60, 384), F32)
    for k in range(4):
        lifted = lax.dot_general(
            lift[:, 60 * k : 60 * k + 60], interior, (((0,), (0,)), ((), ())),
            precision=lax.Precision.HIGHEST, preferred_element_type=F32)
        rest = -(lifted * area[k : k + 1])
        hit = (wide(faces[k : k + 1] - base, 384) == ends).astype(F32).astype(jnp.bfloat16)
        for _ in range(3):
            part = rest.astype(jnp.bfloat16)
            rest = rest - part.astype(F32)
            out = out + lax.dot_general(
                part, hit, (((1,), (1,)), ((), ())), preferred_element_type=F32)
    slab[...] = out
    tsend[...] = jnp.zeros(tsend.shape, F32)
    for s in range(3):
        for k in range(4):
            tsend[s, k, 0] = slab[15 * k : 15 * k + 8, 128 * s : 128 * s + 128]
            tsend[s, k, 1, 0:7] = slab[15 * k + 8 : 15 * k + 15, 128 * s : 128 * s + 128]
    pl.semaphore_wait(bar, len(greeted))
    deliver_start(1)

    for c in loads[5:]:
        c.wait()
    dg[...] = jnp.zeros(dg.shape, F32)
    dg[0] = diag[0:8] - SHIFT
    dg[1, 0:7] = diag[8:15] - SHIFT

    blk[...] = jnp.zeros(blk.shape, F32)

    def respace(n, carry):
        s, i = n // 15, lax.rem(n, 15)
        for k in range(4):
            blk[s, i, 2 * k] = raw[s, i, 15 * k : 15 * k + 8]
            blk[s, i, 2 * k + 1, 0:7] = raw[s, i, 15 * k + 8 : 15 * k + 15]
        return carry

    lax.fori_loop(0, slots * 15, respace, 0)
    numbers = lax.broadcasted_iota(jnp.int32, (8, 128), 1).astype(F32) + 1.0
    numbers = numbers.astype(jnp.bfloat16)
    for s in range(1, slots):
        row = cols[s : s + 1]
        there = jnp.where(row >= 0, row - base, -1)
        lanes_of[s - 1] = wide(there & 127, 8)
        part_of[s - 1] = wide(there >> 7, 8)
        hit = (wide(there, 384) == ends).astype(F32).astype(jnp.bfloat16)
        found = lax.dot_general(
            numbers, hit, (((1,), (1,)), ((), ())), preferred_element_type=F32)
        found = found.astype(jnp.int32) - 1
        for k in range(3):
            back[s - 1, k] = found[:, 128 * k : 128 * k + 128]

    def spread8(value):
        return jnp.broadcast_to(value[None], (8, 8, 128)).reshape(64, 128)

    def operate(par, v):
        vrecv[par, 1, g] = v
        for s, h in LINKS:
            v_copy(par, s, h).start()
        rows = v.reshape(16, 128)
        vb = jnp.concatenate([wide(rows[i : i + 1], 8)[None] for i in range(15)], axis=0)
        outs = [None, None, None]
        for s in range(slots):
            turned = jnp.sum(blk[s] * vb[:, None], axis=0).reshape(64, 128)
            if s == 0:
                outs[1] = turned
                continue
            for k in range(3):
                lane = back[s - 1, k]
                moved = pick(turned, spread8(lane & 127))
                moved = jnp.where(spread8(lane) >= 0, moved, 0.0)
                outs[k] = moved if outs[k] is None else outs[k] + moved
        for k in range(3):
            tsend[k] = outs[k].reshape(4, 2, 8, 128)
        deliver_start(par)
        for s, h in LINKS:
            v_from(par, s, h).wait_recv()
        parts = [vrecv[par, k].reshape(64, 128) for k in range(3)]
        acc = jnp.zeros((15, 8, 128), F32)
        for s in range(slots):
            if s == 0:
                taken = parts[1]
            else:
                lane, part = spread8(lanes_of[s - 1]), spread8(part_of[s - 1])
                taken = jnp.zeros((64, 128), F32)
                for k in range(3):
                    taken = jnp.where(part == k, pick(parts[k], lane), taken)
            acc = acc + jnp.sum(blk[s] * taken.reshape(1, 8, 8, 128), axis=1)
        rows = jnp.concatenate([jnp.sum(acc, axis=1), jnp.zeros((1, 128), F32)], axis=0)
        result = dg[...] * v + rows.reshape(2, 8, 128) + deliver_end(par)
        for s, h in LINKS:
            v_copy(par, s, h).wait_send()
        return result

    me_a, me_b = y * 4 + g, z * 2 + core

    def a_copy(par, n):
        return pltpu.make_async_remote_copy(
            ra.at[par, me_a], ra.at[par, me_a], as_sem.at[n], ar_sem.at[par, me_a],
            device_id=peer_a(*group_a[n]), device_id_type=MESH)

    def a_from(par, n):
        dy, dx = group_a[n]
        src = lax.rem(y + 4 - dy, 4) * 4 + lax.rem(g + 4 - dx, 4)
        return pltpu.make_async_remote_copy(
            ra.at[par, me_a], ra.at[par, src], as_sem.at[n], ar_sem.at[par, src],
            device_id=peer_a(dy, dx), device_id_type=MESH)

    def b_copy(par, n):
        return pltpu.make_async_remote_copy(
            rb.at[par, me_b], rb.at[par, me_b], bs_sem.at[n], br_sem.at[par, me_b],
            device_id=peer_b(*group_b[n]), device_id_type=MESH)

    def b_from(par, n):
        dz, dc = group_b[n]
        src = lax.rem(z + zs - dz, zs) * 2 + lax.rem(core + 2 - dc, 2)
        return pltpu.make_async_remote_copy(
            rb.at[par, me_b], rb.at[par, src], bs_sem.at[n], br_sem.at[par, src],
            device_id=peer_b(dz, dc), device_id_type=MESH)

    T0, T1, T2, G0, G1, G2, G3, X, CUR = range(9)

    def sum_start(par):
        basis = [st[T0], st[G0], st[T1], st[G1], st[T2] + st[G2]]
        items = [basis[i] * basis[j] for i in range(5) for j in range(i, 5)] + [dg[...]]
        both = jnp.concatenate([(a[0] + a[1])[None] for a in items], axis=0)
        flat = jnp.sum(jnp.sum(both, axis=1), axis=1, keepdims=True)
        keep = lax.broadcasted_iota(jnp.int32, (16, 128), 0) == lax.broadcasted_iota(
            jnp.int32, (16, 128), 1)
        row = jnp.sum(jnp.where(keep, jnp.broadcast_to(flat, (16, 128)), 0.0), axis=0, keepdims=True)
        ra[par, me_a] = row
        for n in range(len(group_a)):
            a_copy(par, n).start()

    def sum_middle(par):
        for n in range(len(group_a)):
            a_from(par, n).wait_recv()
        rb[par, me_b] = jnp.sum(ra[par], axis=0)
        for n in range(len(group_b)):
            b_copy(par, n).start()
        for n in range(len(group_a)):
            a_copy(par, n).wait_send()

    def sum_end(par):
        for n in range(len(group_b)):
            b_from(par, n).wait_recv()
        total = jnp.sum(rb[par], axis=0)
        for n in range(len(group_b)):
            b_copy(par, n).wait_send()
        return [jnp.broadcast_to(total[:, n : n + 1], (8, 128)) for n in range(16)]

    def two_steps(total):
        shift = cs[...]
        gram = {}
        n = 0
        for i in range(5):
            for j in range(i, 5):
                gram[i, j] = gram[j, i] = total[n]
                n += 1

        def form(a, b):
            whole = None
            for i, left in a.items():
                inner = None
                for j, right in b.items():
                    term = gram[i, j] * right
                    inner = term if inner is None else inner + term
                inner = left * inner
                whole = inner if whole is None else whole + inner
            return whole

        rr0 = gram[0, 0]
        pp = gram[0, 0] + 2.0 * gram[0, 1] + gram[1, 1]
        pbp = gram[0, 2] + gram[0, 3] + gram[1, 2] + gram[1, 3]
        al0 = rr0 / (shift * pp + pbp)
        b, e = -(al0 * shift), -al0
        a = 1.0 + b
        r1 = {0: a, 1: b, 2: e, 3: e}
        rr1 = form(r1, r1)
        be0 = rr1 / rr0
        pa, pb = a + be0, b + be0
        p1 = {0: pa, 1: pb, 2: e, 3: e}
        bp1 = {2: pa, 3: pb, 4: e}
        al1 = rr1 / (shift * form(p1, p1) + form(p1, bp1))
        sc = al1 * shift
        tail = e * (1.0 - sc)
        r2 = {0: a - sc * pa, 1: b - sc * pb, 2: tail - al1 * pa, 3: tail - al1 * pb, 4: -(al1 * e)}
        be1 = form(r2, r2) / rr1
        x0, x1 = al0 + al1 * pa, al0 + al1 * pb
        return r2, (be1 * pa, be1 * pb, be1 * e), (x0, x1, al1 * e)

    r0 = deliver_end(1)
    for n in range(9):
        st[n] = jnp.zeros((2, 8, 128), F32)
    st[T0] = r0
    st[CUR] = r0

    def outer(o, carry):
        par = lax.rem(o, 2)
        sum_start(par)
        first = operate(0, st[CUR])
        sum_middle(par)
        second = operate(1, first + st[G3])
        total = sum_end(par)

        @pl.when(o == 0)
        def _():
            move = total[15] * (1.0 / (60.0 * faces_all))
            cs[...] = move + SHIFT
            inside = lax.broadcasted_iota(jnp.int32, (2, 8, 128), 0) * 8 + lax.broadcasted_iota(
                jnp.int32, (2, 8, 128), 1) < 15
            dg[...] = jnp.where(inside, dg[...] - move[None], 0.0)
            t0 = st[T0]
            t1 = first - move * t0
            t2 = second - move * (first + t1)
            st[T1], st[T2], st[CUR] = t1, t2, t2

        @pl.when(o > 0)
        def _():
            r2, gg, xx = two_steps(total)
            t = [st[T0], st[T1], st[T2], first]
            q = [st[G0], st[G1], st[G2], st[G3]]
            h = [None, t[1] + q[1], t[2] + q[2], t[3] + q[3], second]
            st[X] = st[X] + xx[0] * t[0] + xx[1] * q[0] + xx[2] * h[1]
            for k, n in enumerate((T0, T1, T2)):
                new = (r2[4] * h[k + 2] + r2[2] * t[k + 1] + r2[3] * q[k + 1]
                       + r2[0] * t[k] + r2[1] * q[k])
                st[n] = new
                if n == T2:
                    st[CUR] = new
            for k, n in enumerate((G0, G1, G2, G3)):
                st[n] = gg[2] * h[k + 1] + gg[0] * t[k] + gg[1] * q[k]

        return carry

    lax.fori_loop(0, 4, outer, 0)
    sum_start(0)
    sum_middle(0)
    r2, gg, xx = two_steps(sum_end(0))
    t, q = [st[T0], st[T1], st[T2]], [st[G0], st[G1], st[G2]]
    x = st[X] + xx[0] * t[0] + xx[1] * q[0] + xx[2] * (t[1] + q[1])
    r = (r2[4] * (t[2] + q[2]) + r2[2] * t[1] + r2[3] * q[1] + r2[0] * t[0] + r2[1] * q[0])
    sol_ref[...] = x.reshape(16, 128)[0:15]
    res_ref[...] = r.reshape(16, 128)[0:15]


def solution(mesh):
    n_dom, n_grp = mesh.shape["dom"], mesh.shape["grp"]

    def on_device(element_faces, interior_load, inverses, lift_operator, face_area, columns, blocks, diagonal):
        args = (element_faces, interior_load, inverses, lift_operator, face_area, columns, blocks, diagonal)
        order = (0, 1, 2, 3, 4, 5, 6, 7)
        slots, zs = columns.shape[0], n_dom // 8
        dma, vmem = pltpu.SemaphoreType.DMA, pltpu.VMEM
        faces_all = float(diagonal.shape[1] * n_dom)

        def body(*refs):
            kernel(n_dom, n_grp, faces_all, *refs)

        return pl.pallas_call(
            body,
            out_shape=(jax.ShapeDtypeStruct(diagonal.shape, F32),) * 2,
            in_specs=[pl.BlockSpec(memory_space=pl.ANY)] * 8,
            out_specs=(pl.BlockSpec(memory_space=pltpu.VMEM),) * 2,
            scratch_shapes=[vmem(args[i].shape, args[i].dtype) for i in order]
            + [
                vmem((slots, 15, 8, 8, 128), F32),
                vmem((2, 8, 128), F32),
                vmem((slots - 1, 8, 128), jnp.int32),
                vmem((slots - 1, 8, 128), jnp.int32),
                vmem((slots - 1, 3, 8, 128), jnp.int32),
                vmem((60, 384), F32),
                vmem((2, 3, 4, 2, 8, 128), F32),
                vmem((3, 4, 2, 8, 128), F32),
                vmem((2, 3, 4, 2, 8, 128), F32),
                vmem((2, 16, 1, 128), F32),
                vmem((2, 2 * zs, 1, 128), F32),
                vmem((9, 2, 8, 128), F32),
                vmem((8, 128), F32),
                dma((8,)), dma((3, 4)), dma((2, 3, 4)), dma((3, 4)), dma((2, 3, 4)),
                dma((15,)), dma((2, 16)), dma((2 * zs - 1,)), dma((2, 2 * zs)),
            ],
            compiler_params=pltpu.CompilerParams(
                collective_id=0, has_side_effects=True, vmem_limit_bytes=40 * 1024 * 1024),
            name="cg",
        )(*args)

    return jax.shard_map(
        on_device,
        mesh=mesh,
        in_specs=(
            P(None, "dom"), P(None, "dom"), P("grp", None, "dom"), P("grp", None), P(None, "dom"),
            P(None, "dom"), P(None, "grp", None, "dom"), P("grp", "dom"),
        ),
        out_specs=(P("grp", "dom"), P("grp", "dom")),
        check_vma=False,
    )
```

```python
import jax
import jax.numpy as jnp
from jax import lax
from jax.experimental import pallas as pl
from jax.experimental.pallas import tpu as pltpu
from jax.sharding import PartitionSpec as P

MESH = pl.DeviceIdType.MESH
F32 = jnp.float32
SHIFT = 1.16
FAR_FIRST = (2, 1, 3, 0)
NEAR_FIRST = (0, 1, 3, 2)
LINKS = [(s, h) for h in FAR_FIRST for s in (1, -1)] + [(0, 2), (0, 1), (0, 3)]


def wide(row, rows):
    return jnp.broadcast_to(row, (rows, row.shape[-1]))


def pick(value, lanes):
    return jnp.take_along_axis(value, lanes, axis=1, mode="promise_in_bounds")


def kernel(
    n_dom, n_grp, faces_all,
    faces_h, load_h, inv_h, lift_h, area_h, cols_h, raw_h, diag_h,
    sol_ref, res_ref,
    faces, load, inv, lift, area, cols, raw, diag,
    blk, dg, lanes_of, part_of, back, slab, vrecv, tsend, trecv, ra, rb, st, cs, cf,
    in_sem, vs_sem, vr_sem, ts_sem, tr_sem, as_sem, ar_sem, bs_sem, br_sem,
):
    d, g = lax.axis_index("dom"), lax.axis_index("grp")
    core = lax.rem(d, 2)
    y = lax.rem(d // 2, 4)
    z = d // 8
    zs = n_dom // 8
    slots = blk.shape[0]

    loads = [
        pltpu.make_async_copy(a, b, in_sem.at[i])
        for i, (a, b) in enumerate(
            [(inv_h, inv), (load_h, load), (lift_h, lift), (area_h, area), (faces_h, faces),
             (cols_h, cols), (diag_h, diag), (raw_h, raw)]
        )
    ]
    for c in loads:
        c.start()

    def link(s, h):
        return lax.rem(d + s + n_dom, n_dom), lax.rem(g + h, n_grp)

    def peer_a(dy, dx, c):
        return (z * 4 + lax.rem(y + dy, 4)) * 2 + c, lax.rem(g + dx, 4)

    def peer_b(dz, c):
        return (lax.rem(z + dz, zs) * 4 + y) * 2 + c, g

    group_a = [(a, b) for a in range(4) for b in range(4)]
    bar = pltpu.get_barrier_semaphore()

    def greet(who):
        pl.semaphore_signal(bar, inc=1, device_id=who, device_id_type=MESH)

    for s, h in LINKS:
        greet(link(s, h))
    for a, b in group_a[1:]:
        greet(peer_a(a, b, 1))
    for a in range(1, zs):
        greet(peer_b(a, 1))

    @pl.when(core == 0)
    def _():
        greet(peer_a(0, 0, 1))
        greet(peer_b(0, 1))

    @pl.when(core == 1)
    def _():
        for a, b in group_a:
            greet(peer_a(a, b, 0))
        for a in range(zs):
            greet(peer_b(a, 0))

    greetings = len(LINKS) + 16 + zs + core * (14 + zs)

    def t_copy(par, s, h):
        peer = link(s, h)
        return pltpu.make_async_remote_copy(
            tsend.at[s + 1, peer[1]], trecv.at[par, s + 1, g], ts_sem.at[s + 1, h],
            tr_sem.at[par, s + 1, g], device_id=peer, device_id_type=MESH)

    def t_from(par, s, h):
        src = lax.rem(g + n_grp - h, n_grp)
        return pltpu.make_async_remote_copy(
            tsend.at[s + 1, g], trecv.at[par, s + 1, src], ts_sem.at[s + 1, h],
            tr_sem.at[par, s + 1, src], device_id=link(s, h), device_id_type=MESH)

    def v_copy(par, s, h):
        return pltpu.make_async_remote_copy(
            vrecv.at[par, 1, g], vrecv.at[par, 1 - s, g], vs_sem.at[s + 1, h],
            vr_sem.at[par, 1 - s, g], device_id=link(s, h), device_id_type=MESH)

    def v_from(par, s, h):
        src = lax.rem(g + n_grp - h, n_grp)
        return pltpu.make_async_remote_copy(
            vrecv.at[par, 1, g], vrecv.at[par, 1 - s, src], vs_sem.at[s + 1, h],
            vr_sem.at[par, 1 - s, src], device_id=link(s, h), device_id_type=MESH)

    def deliver_start(par):
        trecv[par, 1, g] = tsend[1, g]
        for s, h in LINKS:
            t_copy(par, s, h).start()

    def deliver_end(par):
        for s, h in LINKS:
            t_from(par, s, h).wait_recv()
        total = trecv[par, 0, 0]
        for s in range(3):
            for k in range(4):
                if (s, k) != (0, 0):
                    total = total + trecv[par, s, k]
        for s, h in LINKS:
            t_copy(par, s, h).wait_send()
        return total

    for c in loads[:5]:
        c.wait()
    interior = jnp.sum(inv[...].astype(F32) * load[...].astype(F32)[None], axis=1)
    base = (d - 1) * 128
    ends = lax.broadcasted_iota(jnp.int32, (384, 128), 0)
    out = jnp.zeros((60, 384), F32)
    for k in range(4):
        lifted = lax.dot_general(
            lift[:, 60 * k : 60 * k + 60], interior, (((0,), (0,)), ((), ())),
            precision=lax.Precision.HIGHEST, preferred_element_type=F32)
        rest = -(lifted * area[k : k + 1])
        hit = (wide(faces[k : k + 1] - base, 384) == ends).astype(F32).astype(jnp.bfloat16)
        for _ in range(3):
            part = rest.astype(jnp.bfloat16)
            rest = rest - part.astype(F32)
            out = out + lax.dot_general(
                part, hit, (((1,), (1,)), ((), ())), preferred_element_type=F32)
    slab[...] = out
    tsend[...] = jnp.zeros(tsend.shape, F32)
    for s in range(3):
        for k in range(4):
            tsend[s, k, 0] = slab[15 * k : 15 * k + 8, 128 * s : 128 * s + 128]
            tsend[s, k, 1, 0:7] = slab[15 * k + 8 : 15 * k + 15, 128 * s : 128 * s + 128]
    pl.semaphore_wait(bar, greetings)
    deliver_start(1)

    for c in loads[5:]:
        c.wait()
    dg[...] = jnp.zeros(dg.shape, F32)
    dg[0] = diag[0:8] - SHIFT
    dg[1, 0:7] = diag[8:15] - SHIFT

    blk[...] = jnp.zeros(blk.shape, F32)

    def respace(n, carry):
        s, i = n // 15, lax.rem(n, 15)
        for k in range(4):
            blk[s, k, i, 0] = raw[s, i, 15 * k : 15 * k + 8]
            blk[s, k, i, 1, 0:7] = raw[s, i, 15 * k + 8 : 15 * k + 15]
        return carry

    lax.fori_loop(0, slots * 15, respace, 0)
    numbers = lax.broadcasted_iota(jnp.int32, (8, 128), 1).astype(F32) + 1.0
    numbers = numbers.astype(jnp.bfloat16)
    for s in range(1, slots):
        row = cols[s : s + 1]
        there = jnp.where(row >= 0, row - base, -1)
        lanes_of[s - 1] = wide(there & 127, 8)
        part_of[s - 1] = wide(there >> 7, 8)
        hit = (wide(there, 384) == ends).astype(F32).astype(jnp.bfloat16)
        found = lax.dot_general(
            numbers, hit, (((1,), (1,)), ((), ())), preferred_element_type=F32)
        found = found.astype(jnp.int32) - 1
        for k in range(3):
            back[s - 1, k] = found[:, 128 * k : 128 * k + 128]

    def twice(value):
        return jnp.broadcast_to(value[None], (2, 8, 128)).reshape(16, 128)

    def operate(par, v, during, late):
        vrecv[par, 1, g] = v
        for s, h in LINKS:
            v_copy(par, s, h).start()
        rows = v.reshape(16, 128)
        vb = jnp.concatenate([wide(rows[i : i + 1], 8)[None] for i in range(15)], axis=0)
        for h in FAR_FIRST:
            k = lax.rem(g + h, n_grp)
            outs = [None, None, None]
            for s in range(slots):
                turned = jnp.sum(blk[s, k] * vb[:, None], axis=0).reshape(16, 128)
                if s == 0:
                    outs[1] = turned
                    continue
                for p in range(3):
                    lane = back[s - 1, p]
                    moved = pick(turned, twice(lane & 127))
                    moved = jnp.where(twice(lane) >= 0, moved, 0.0)
                    outs[p] = moved if outs[p] is None else outs[p] + moved
            for p in range(3):
                tsend[p, k] = outs[p].reshape(2, 8, 128)
            if h == 0:
                trecv[par, 1, g] = outs[1].reshape(2, 8, 128)
            for s in (1, -1, 0):
                if (s, h) != (0, 0):
                    t_copy(par, s, h).start()
        during()
        acc = jnp.zeros((15, 8, 128), F32)
        for h in NEAR_FIRST:
            k = lax.rem(g + h, n_grp)
            for s in (0, 1, -1):
                if (s, h) != (0, 0):
                    v_from(par, s, (n_grp - h) % n_grp).wait_recv()
            parts = [vrecv[par, p, k].reshape(16, 128) for p in range(3)]
            for s in range(slots):
                if s == 0:
                    taken = parts[1]
                else:
                    lane, part = twice(lanes_of[s - 1]), twice(part_of[s - 1])
                    taken = jnp.zeros((16, 128), F32)
                    for p in range(3):
                        taken = jnp.where(part == p, pick(parts[p], lane), taken)
                acc = acc + jnp.sum(blk[s, k] * taken.reshape(1, 2, 8, 128), axis=1)
        rows = jnp.concatenate([jnp.sum(acc, axis=1), jnp.zeros((1, 128), F32)], axis=0)
        result = dg[...] * v + rows.reshape(2, 8, 128)
        late()
        result = result + deliver_end(par)
        for s, h in LINKS:
            v_copy(par, s, h).wait_send()
        return result

    me_a = (y * 4 + g) * 2 + core

    def a_copy(par, n):
        dy, dx = group_a[n]
        return pltpu.make_async_remote_copy(
            ra.at[par, me_a], ra.at[par, me_a], as_sem.at[n], ar_sem.at[par, me_a],
            device_id=peer_a(dy, dx, 1), device_id_type=MESH)

    def a_from(par, n, c):
        dy, dx = group_a[n]
        src = (lax.rem(y + 4 - dy, 4) * 4 + lax.rem(g + 4 - dx, 4)) * 2 + c
        return pltpu.make_async_remote_copy(
            ra.at[par, me_a], ra.at[par, src], as_sem.at[n], ar_sem.at[par, src],
            device_id=peer_a(dy, dx, 1), device_id_type=MESH)

    def b_copy(par, dz, c):
        return pltpu.make_async_remote_copy(
            rb.at[par, z], rb.at[par, z], bs_sem.at[c, dz], br_sem.at[par, z],
            device_id=peer_b(dz, c), device_id_type=MESH)

    def b_from(par, dz):
        src = lax.rem(z + zs - dz, zs)
        return pltpu.make_async_remote_copy(
            rb.at[par, z], rb.at[par, src], bs_sem.at[0, dz], br_sem.at[par, src],
            device_id=peer_b(dz, 1 - core), device_id_type=MESH)

    T0, T1, T2, G0, G1, G2, G3, X, CUR, FIRST, SECOND = range(11)

    def sum_start(par):
        basis = [st[T0], st[G0], st[T1], st[G1], st[T2] + st[G2]]
        items = [basis[i] * basis[j] for i in range(5) for j in range(i, 5)] + [dg[...]]
        both = jnp.concatenate([(a[0] + a[1])[None] for a in items], axis=0)
        flat = jnp.sum(jnp.sum(both, axis=1), axis=1, keepdims=True)
        keep = lax.broadcasted_iota(jnp.int32, (16, 128), 0) == lax.broadcasted_iota(
            jnp.int32, (16, 128), 1)
        row = jnp.sum(jnp.where(keep, jnp.broadcast_to(flat, (16, 128)), 0.0), axis=0, keepdims=True)
        ra[par, me_a] = row
        for n in range(1, 16):
            a_copy(par, n).start()

        @pl.when(core == 0)
        def _():
            a_copy(par, 0).start()

    def sum_middle(par):
        @pl.when(core == 1)
        def _():
            for n in range(16):
                a_from(par, n, 0).wait_recv()
                if n:
                    a_from(par, n, 1).wait_recv()
            rb[par, z] = jnp.sum(ra[par], axis=0)
            for n in range(1, zs):
                b_copy(par, n, 0).start()
                b_copy(par, n, 1).start()
            b_copy(par, 0, 0).start()

        for n in range(1, 16):
            a_copy(par, n).wait_send()

        @pl.when(core == 0)
        def _():
            a_copy(par, 0).wait_send()

    def sum_end(par):
        for n in range(1, zs):
            b_from(par, n).wait_recv()

        @pl.when(core == 0)
        def _():
            b_from(par, 0).wait_recv()

        total = jnp.sum(rb[par], axis=0)

        @pl.when(core == 1)
        def _():
            for n in range(1, zs):
                b_copy(par, n, 0).wait_send()
                b_copy(par, n, 1).wait_send()
            b_copy(par, 0, 0).wait_send()

        return [jnp.broadcast_to(total[:, n : n + 1], (8, 128)) for n in range(16)]

    def two_steps(total):
        shift = cs[...]
        gram = {}
        n = 0
        for i in range(5):
            for j in range(i, 5):
                gram[i, j] = gram[j, i] = total[n]
                n += 1

        def form(a, b):
            whole = None
            for i, left in a.items():
                inner = None
                for j, right in b.items():
                    term = gram[i, j] * right
                    inner = term if inner is None else inner + term
                inner = left * inner
                whole = inner if whole is None else whole + inner
            return whole

        rr0 = gram[0, 0]
        pp = gram[0, 0] + 2.0 * gram[0, 1] + gram[1, 1]
        pbp = gram[0, 2] + gram[0, 3] + gram[1, 2] + gram[1, 3]
        al0 = rr0 / (shift * pp + pbp)
        b, e = -(al0 * shift), -al0
        a = 1.0 + b
        r1 = {0: a, 1: b, 2: e, 3: e}
        rr1 = form(r1, r1)
        be0 = rr1 / rr0
        pa, pb = a + be0, b + be0
        p1 = {0: pa, 1: pb, 2: e, 3: e}
        bp1 = {2: pa, 3: pb, 4: e}
        al1 = rr1 / (shift * form(p1, p1) + form(p1, bp1))
        sc = al1 * shift
        tail = e * (1.0 - sc)
        r2 = {0: a - sc * pa, 1: b - sc * pb, 2: tail - al1 * pa, 3: tail - al1 * pb, 4: -(al1 * e)}
        be1 = form(r2, r2) / rr1
        x0, x1 = al0 + al1 * pa, al0 + al1 * pb
        return r2, (be1 * pa, be1 * pb, be1 * e), (x0, x1, al1 * e)

    def advance():
        c = [cf[n] for n in range(11)]
        t = [st[T0], st[T1], st[T2], st[FIRST]]
        q = [st[G0], st[G1], st[G2], st[G3]]
        h = [None, t[1] + q[1], t[2] + q[2], t[3] + q[3], st[SECOND]]
        st[X] = st[X] + c[8] * t[0] + c[9] * q[0] + c[10] * h[1]
        for k, n in enumerate((T0, T1)):
            st[n] = (c[4] * h[k + 2] + c[2] * t[k + 1] + c[3] * q[k + 1]
                     + c[0] * t[k] + c[1] * q[k])
        st[T2] = st[CUR]
        for k, n in enumerate((G0, G1, G2, G3)):
            st[n] = c[7] * h[k + 1] + c[5] * t[k] + c[6] * q[k]

    r0 = deliver_end(1)
    for n in range(11):
        st[n] = jnp.zeros((2, 8, 128), F32)
        cf[n] = jnp.zeros((8, 128), F32)
    cf[0] = jnp.ones((8, 128), F32)
    st[T0] = r0
    st[CUR] = r0

    def outer(o, carry):
        par = lax.rem(o, 2)

        def open_sum():
            advance()
            sum_start(par)

        def close_sum():
            total = sum_end(par)

            @pl.when(o == 0)
            def _():
                cs[...] = total[15] * (1.0 / (60.0 * faces_all)) + SHIFT

            @pl.when(o > 0)
            def _():
                r2, gg, xx = two_steps(total)
                for n in range(5):
                    cf[n] = r2[n]
                for n in range(3):
                    cf[5 + n] = gg[n]
                    cf[8 + n] = xx[n]

        first = operate(0, st[CUR], open_sum, lambda: None)
        st[FIRST] = first
        second = operate(1, first + st[G3], lambda: sum_middle(par), close_sum)
        st[SECOND] = second

        @pl.when(o == 0)
        def _():
            move = cs[...] - SHIFT
            inside = lax.broadcasted_iota(jnp.int32, (2, 8, 128), 0) * 8 + lax.broadcasted_iota(
                jnp.int32, (2, 8, 128), 1) < 15
            dg[...] = jnp.where(inside, dg[...] - move[None], 0.0)
            t0 = st[T0]
            t1 = first - move * t0
            t2 = second - move * (first + t1)
            st[T1], st[CUR] = t1, t2
            st[T2] = t2

        @pl.when(o > 0)
        def _():
            st[CUR] = (cf[4] * second + cf[2] * first + cf[3] * st[G3]
                       + cf[0] * st[T2] + cf[1] * st[G2])

        return carry

    lax.fori_loop(0, 4, outer, 0)
    advance()
    sum_start(0)
    sum_middle(0)
    r2, gg, xx = two_steps(sum_end(0))
    t, q = [st[T0], st[T1], st[T2]], [st[G0], st[G1], st[G2]]
    x = st[X] + xx[0] * t[0] + xx[1] * q[0] + xx[2] * (t[1] + q[1])
    r = (r2[4] * (t[2] + q[2]) + r2[2] * t[1] + r2[3] * q[1] + r2[0] * t[0] + r2[1] * q[0])
    sol_ref[...] = x.reshape(16, 128)[0:15]
    res_ref[...] = r.reshape(16, 128)[0:15]


def solution(mesh):
    n_dom, n_grp = mesh.shape["dom"], mesh.shape["grp"]

    def on_device(element_faces, interior_load, inverses, lift_operator, face_area, columns, blocks, diagonal):
        args = (element_faces, interior_load, inverses, lift_operator, face_area, columns, blocks, diagonal)
        order = (0, 1, 2, 3, 4, 5, 6, 7)
        slots, zs = columns.shape[0], n_dom // 8
        dma, vmem = pltpu.SemaphoreType.DMA, pltpu.VMEM
        faces_all = float(diagonal.shape[1] * n_dom)

        def body(*refs):
            kernel(n_dom, n_grp, faces_all, *refs)

        found = pl.pallas_call(
            body,
            out_shape=(jax.ShapeDtypeStruct(diagonal.shape, F32),) * 2,
            in_specs=[pl.BlockSpec(memory_space=pl.ANY)] * 8,
            out_specs=(pl.BlockSpec(memory_space=pltpu.VMEM),) * 2,
            scratch_shapes=[vmem(args[i].shape, args[i].dtype) for i in order]
            + [
                vmem((slots, n_grp, 15, 2, 8, 128), F32),
                vmem((2, 8, 128), F32),
                vmem((slots - 1, 8, 128), jnp.int32),
                vmem((slots - 1, 8, 128), jnp.int32),
                vmem((slots - 1, 3, 8, 128), jnp.int32),
                vmem((60, 384), F32),
                vmem((2, 3, 4, 2, 8, 128), F32),
                vmem((3, 4, 2, 8, 128), F32),
                vmem((2, 3, 4, 2, 8, 128), F32),
                vmem((2, 32, 1, 128), F32),
                vmem((2, zs, 1, 128), F32),
                vmem((11, 2, 8, 128), F32),
                vmem((8, 128), F32),
                vmem((11, 8, 128), F32),
                dma((8,)), dma((3, 4)), dma((2, 3, 4)), dma((3, 4)), dma((2, 3, 4)),
                dma((16,)), dma((2, 32)), dma((2, zs)), dma((2, zs)),
            ],
            compiler_params=pltpu.CompilerParams(
                collective_id=0, has_side_effects=True, vmem_limit_bytes=62 * 1024 * 1024),
            name="cg",
        )(*args)

        def hand_over(x, r, x_out, r_out, sem):
            moves = [pltpu.make_async_copy(x, x_out, sem.at[0]), pltpu.make_async_copy(r, r_out, sem.at[1])]
            for m in moves:
                m.start()
            for m in moves:
                m.wait()

        return pl.pallas_call(
            hand_over,
            out_shape=(jax.ShapeDtypeStruct(diagonal.shape, F32),) * 2,
            in_specs=[pl.BlockSpec(memory_space=pl.ANY)] * 2,
            out_specs=(pl.BlockSpec(memory_space=pl.ANY),) * 2,
            scratch_shapes=[dma((2,))],
            name="hand_over",
        )(*found)

    return jax.shard_map(
        on_device,
        mesh=mesh,
        in_specs=(
            P(None, "dom"), P(None, "dom"), P("grp", None, "dom"), P("grp", None), P(None, "dom"),
            P(None, "dom"), P(None, "grp", None, "dom"), P("grp", "dom"),
        ),
        out_specs=(P("grp", "dom"), P("grp", "dom")),
        check_vma=False,
    )
```

```python
import jax
import jax.numpy as jnp
from jax import lax
from jax.experimental import pallas as pl
from jax.experimental.pallas import tpu as pltpu
from jax.sharding import PartitionSpec as P

MESH = pl.DeviceIdType.MESH
F32 = jnp.float32
SHIFT = 1.16
FAR_FIRST = (2, 1, 3, 0)
A_ORDER = (10, 9, 11, 6, 14, 5, 7, 13, 15, 8, 2, 4, 12, 1, 3)
OUT, IN, OWN = 1, -1, 0
LINKS = [(OUT, h) for h in FAR_FIRST] + [(IN, h) for h in FAR_FIRST] + [(OWN, 2), (OWN, 1), (OWN, 3)]


def wide(row, rows):
    return jnp.broadcast_to(row, (rows, row.shape[-1]))


def pick(value, lanes):
    return jnp.take_along_axis(value, lanes, axis=1, mode="promise_in_bounds")


def kernel(
    n_dom, n_grp, faces_all,
    faces_h, load_h, inv_h, lift_h, area_h, cols_h, raw_h, diag_h,
    sol_ref, res_ref,
    faces, load, inv, lift, area, cols, raw, diag,
    blk, dg, lanes_of, part_of, back, slab, vrecv, tsend, trecv, hold, ra, rb, st, cs, cf,
    in_sem, vs_sem, vr_sem, ts_sem, tr_sem, as_sem, ar_sem, bs_sem, br_sem,
):
    d, g = lax.axis_index("dom"), lax.axis_index("grp")
    core = lax.rem(d, 2)
    y = lax.rem(d // 2, 4)
    z = d // 8
    zs = n_dom // 8
    slots = blk.shape[0]

    loads = [
        pltpu.make_async_copy(a, b, in_sem.at[i])
        for i, (a, b) in enumerate(
            [(inv_h, inv), (load_h, load), (lift_h, lift), (area_h, area), (faces_h, faces),
             (cols_h, cols), (diag_h, diag), (raw_h, raw)]
        )
    ]
    for c in loads:
        c.start()

    away = 2 * core - 1

    def link(s, h):
        s = s * away
        return lax.rem(d + s + n_dom, n_dom), lax.rem(g + h, n_grp)

    def peer_a(dy, dx, c):
        return (z * 4 + lax.rem(y + dy, 4)) * 2 + c, lax.rem(g + dx, 4)

    def peer_b(dz, c):
        return (lax.rem(z + dz, zs) * 4 + y) * 2 + c, g

    group_a = [(a, b) for a in range(4) for b in range(4)]
    b_order = sorted(range(1, zs), key=lambda n: -min(n, zs - n))
    ends_low, ends_high = (3 - g) // 3, g // 3
    far = [2 + ends_low, 3 - ends_low - 2 * ends_high]
    far = far + [6 - far[0] - far[1], 0]
    near = far[::-1]
    bar = pltpu.get_barrier_semaphore()

    def greet(who):
        pl.semaphore_signal(bar, inc=1, device_id=who, device_id_type=MESH)

    for s, h in LINKS:
        greet(link(s, h))
    for a, b in group_a[1:]:
        greet(peer_a(a, b, 1))
    for a in range(1, zs):
        greet(peer_b(a, 1))

    @pl.when(core == 0)
    def _():
        greet(peer_a(0, 0, 1))
        greet(peer_b(0, 1))

    @pl.when(core == 1)
    def _():
        for a, b in group_a:
            greet(peer_a(a, b, 0))
        for a in range(zs):
            greet(peer_b(a, 0))

    greetings = len(LINKS) + 16 + zs + core * (14 + zs)

    def t_copy(par, s, h):
        peer = link(s, h)
        s = s * away
        return pltpu.make_async_remote_copy(
            tsend.at[s + 1, peer[1]], trecv.at[par, s + 1, g], ts_sem.at[s + 1, h],
            tr_sem.at[par, s + 1, g], device_id=peer, device_id_type=MESH)

    def t_from(par, s, h):
        src, peer = lax.rem(g + n_grp - h, n_grp), link(s, h)
        s = -s * away
        return pltpu.make_async_remote_copy(
            tsend.at[s + 1, g], trecv.at[par, s + 1, src], ts_sem.at[s + 1, h],
            tr_sem.at[par, s + 1, src], device_id=peer, device_id_type=MESH)

    def v_copy(par, s, h):
        peer = link(s, h)
        s = s * away
        return pltpu.make_async_remote_copy(
            vrecv.at[par, 1, g], vrecv.at[par, 1 - s, g], vs_sem.at[s + 1, h],
            vr_sem.at[par, 1 - s, g], device_id=peer, device_id_type=MESH)

    def v_from(par, s, h):
        src, peer = lax.rem(g + n_grp - h, n_grp), link(s, h)
        s = s * away
        return pltpu.make_async_remote_copy(
            vrecv.at[par, 1, g], vrecv.at[par, 1 + s, src], vs_sem.at[s + 1, h],
            vr_sem.at[par, 1 + s, src], device_id=peer, device_id_type=MESH)

    def deliver_start(par):
        trecv[par, 1, g] = tsend[1, g]
        for s, h in LINKS:
            t_copy(par, s, h).start()

    def deliver_end(par):
        for s, h in LINKS:
            t_from(par, s, h).wait_recv()
        total = trecv[par, 0, 0]
        for s in range(3):
            for k in range(4):
                if (s, k) != (0, 0):
                    total = total + trecv[par, s, k]
        for s, h in LINKS:
            t_copy(par, s, h).wait_send()
        return total

    for c in loads[:5]:
        c.wait()
    interior = jnp.sum(inv[...].astype(F32) * load[...].astype(F32)[None], axis=1)
    base = (d - 1) * 128
    ends = lax.broadcasted_iota(jnp.int32, (384, 128), 0)
    out = jnp.zeros((60, 384), F32)
    for k in range(4):
        lifted = lax.dot_general(
            lift[:, 60 * k : 60 * k + 60], interior, (((0,), (0,)), ((), ())),
            precision=lax.Precision.HIGHEST, preferred_element_type=F32)
        rest = -(lifted * area[k : k + 1])
        hit = (wide(faces[k : k + 1] - base, 384) == ends).astype(F32).astype(jnp.bfloat16)
        for _ in range(3):
            part = rest.astype(jnp.bfloat16)
            rest = rest - part.astype(F32)
            out = out + lax.dot_general(
                part, hit, (((1,), (1,)), ((), ())), preferred_element_type=F32)
    slab[...] = out
    tsend[...] = jnp.zeros(tsend.shape, F32)
    for s in range(3):
        for k in range(4):
            tsend[s, k, 0] = slab[15 * k : 15 * k + 8, 128 * s : 128 * s + 128]
            tsend[s, k, 1, 0:7] = slab[15 * k + 8 : 15 * k + 15, 128 * s : 128 * s + 128]
    pl.semaphore_wait(bar, greetings)
    deliver_start(1)

    for c in loads[5:]:
        c.wait()
    dg[...] = jnp.zeros(dg.shape, F32)
    dg[0] = diag[0:8] - SHIFT
    dg[1, 0:7] = diag[8:15] - SHIFT

    blk[...] = jnp.zeros(blk.shape, F32)

    def respace(n, carry):
        s, i = n // 15, lax.rem(n, 15)
        for k in range(4):
            blk[s, k, i, 0] = raw[s, i, 15 * k : 15 * k + 8]
            blk[s, k, i, 1, 0:7] = raw[s, i, 15 * k + 8 : 15 * k + 15]
        return carry

    lax.fori_loop(0, slots * 15, respace, 0)
    numbers = lax.broadcasted_iota(jnp.int32, (8, 128), 1).astype(F32) + 1.0
    numbers = numbers.astype(jnp.bfloat16)
    for s in range(1, slots):
        row = cols[s : s + 1]
        there = jnp.where(row >= 0, row - base, -1)
        lanes_of[s - 1] = wide(there & 127, 8)
        part_of[s - 1] = wide(there >> 7, 8)
        hit = (wide(there, 384) == ends).astype(F32).astype(jnp.bfloat16)
        found = lax.dot_general(
            numbers, hit, (((1,), (1,)), ((), ())), preferred_element_type=F32)
        found = found.astype(jnp.int32) - 1
        for k in range(3):
            back[s - 1, k] = found[:, 128 * k : 128 * k + 128]

    def twice(value):
        return jnp.broadcast_to(value[None], (2, 8, 128)).reshape(16, 128)

    def scatter(s, turned, p):
        lane = back[s - 1, p]
        moved = pick(turned.reshape(16, 128), twice(lane & 127))
        return jnp.where(twice(lane) >= 0, moved, 0.0).reshape(2, 8, 128)

    def operate(par, v, during, late, early):
        vrecv[par, 1, g] = v
        for h in far[:2]:
            v_copy(par, OUT, h).start()
        rows = v.reshape(16, 128)
        vb = jnp.concatenate([wide(rows[i : i + 1], 8)[None] for i in range(15)], axis=0)
        for h in far:
            k = lax.rem(g + h, n_grp)
            out = None
            for s in range(slots):
                turned = jnp.sum(blk[s, k] * vb[:, None], axis=0)
                hold[s, k] = turned
                if s:
                    moved = scatter(s, turned, 1 + away)
                    out = moved if out is None else out + moved
            tsend[1 + away, k] = out
            t_copy(par, OUT, h).start()
            if h is far[1]:
                v_copy(par, OUT, far[2]).start()
            if h is far[2]:
                v_copy(par, OUT, far[3]).start()
        if early:
            during()
        for h in far:
            k = lax.rem(g + h, n_grp)
            own, inner = hold[0, k], None
            for s in range(1, slots):
                turned = hold[s, k]
                own = own + scatter(s, turned, 1)
                moved = scatter(s, turned, 1 - away)
                inner = moved if inner is None else inner + moved
            tsend[1, k] = own
            tsend[1 - away, k] = inner
            if h is not far[3]:
                v_copy(par, OWN, h).start()
                t_copy(par, OWN, h).start()
            else:
                trecv[par, 1, g] = own
            v_copy(par, IN, h).start()
            t_copy(par, IN, h).start()
        if not early:
            during()
        acc = jnp.zeros((15, 8, 128), F32)
        for h in near:
            k = lax.rem(g + h, n_grp)
            back_h = lax.rem(n_grp - h, n_grp)
            for s in (OWN, IN, OUT):
                if s != OWN or h is not near[0]:
                    v_from(par, s, back_h).wait_recv()
            parts = [vrecv[par, p, k].reshape(16, 128) for p in range(3)]
            for s in range(slots):
                if s == 0:
                    taken = parts[1]
                else:
                    lane, part = twice(lanes_of[s - 1]), twice(part_of[s - 1])
                    taken = jnp.zeros((16, 128), F32)
                    for p in range(3):
                        taken = jnp.where(part == p, pick(parts[p], lane), taken)
                acc = acc + jnp.sum(blk[s, k] * taken.reshape(1, 2, 8, 128), axis=1)
        rows = jnp.concatenate([jnp.sum(acc, axis=1), jnp.zeros((1, 128), F32)], axis=0)
        result = dg[...] * v + rows.reshape(2, 8, 128)
        late()
        for s, h in LINKS:
            t_copy(par, s, h).wait_send()
            v_copy(par, s, h).wait_send()
        result = result + trecv[par, 1, g]
        for kinds in ((OWN, IN), (OUT,)):
            for h in near:
                k = lax.rem(g + h, n_grp)
                for s in kinds:
                    if s != OWN or h is not near[0]:
                        t_from(par, s, lax.rem(n_grp - h, n_grp)).wait_recv()
                        result = result + trecv[par, 1 - s * away, k]
        return result

    me_a = (y * 4 + g) * 2 + core

    def a_copy(par, n):
        dy, dx = group_a[n]
        return pltpu.make_async_remote_copy(
            ra.at[par, me_a], ra.at[par, me_a], as_sem.at[n], ar_sem.at[par, me_a],
            device_id=peer_a(dy, dx, 1), device_id_type=MESH)

    def a_from(par, n, c):
        dy, dx = group_a[n]
        src = (lax.rem(y + 4 - dy, 4) * 4 + lax.rem(g + 4 - dx, 4)) * 2 + c
        return pltpu.make_async_remote_copy(
            ra.at[par, me_a], ra.at[par, src], as_sem.at[n], ar_sem.at[par, src],
            device_id=peer_a(dy, dx, 1), device_id_type=MESH)

    def b_copy(par, dz, c):
        return pltpu.make_async_remote_copy(
            rb.at[par, z], rb.at[par, z], bs_sem.at[c, dz], br_sem.at[par, z],
            device_id=peer_b(dz, c), device_id_type=MESH)

    def b_from(par, dz):
        src = lax.rem(z + zs - dz, zs)
        return pltpu.make_async_remote_copy(
            rb.at[par, z], rb.at[par, src], bs_sem.at[0, dz], br_sem.at[par, src],
            device_id=peer_b(dz, 1 - core), device_id_type=MESH)

    T0, T1, T2, G0, G1, G2, G3, X = range(8)

    def sum_start(par):
        basis = [st[T0], st[G0], st[T1], st[G1], st[T2] + st[G2]]
        items = [basis[i] * basis[j] for i in range(5) for j in range(i, 5)] + [dg[...]]
        both = jnp.concatenate([(a[0] + a[1])[None] for a in items], axis=0)
        flat = jnp.sum(jnp.sum(both, axis=1), axis=1, keepdims=True)
        keep = lax.broadcasted_iota(jnp.int32, (16, 128), 0) == lax.broadcasted_iota(
            jnp.int32, (16, 128), 1)
        row = jnp.sum(jnp.where(keep, jnp.broadcast_to(flat, (16, 128)), 0.0), axis=0, keepdims=True)
        ra[par, me_a] = row
        for n in A_ORDER:
            a_copy(par, n).start()

        @pl.when(core == 0)
        def _():
            a_copy(par, 0).start()

    def sum_middle(par):
        @pl.when(core == 1)
        def _():
            for n in range(16):
                a_from(par, n, 0).wait_recv()
                if n:
                    a_from(par, n, 1).wait_recv()
            rb[par, z] = jnp.sum(ra[par], axis=0)
            for n in b_order:
                b_copy(par, n, 0).start()
                b_copy(par, n, 1).start()
            b_copy(par, 0, 0).start()

        for n in range(1, 16):
            a_copy(par, n).wait_send()

        @pl.when(core == 0)
        def _():
            a_copy(par, 0).wait_send()

    def sum_end(par):
        for n in range(1, zs):
            b_from(par, n).wait_recv()

        @pl.when(core == 0)
        def _():
            b_from(par, 0).wait_recv()

        total = jnp.sum(rb[par], axis=0)

        @pl.when(core == 1)
        def _():
            for n in range(1, zs):
                b_copy(par, n, 0).wait_send()
                b_copy(par, n, 1).wait_send()
            b_copy(par, 0, 0).wait_send()

        return [jnp.broadcast_to(total[:, n : n + 1], (8, 128)) for n in range(16)]

    def two_steps(total):
        shift = cs[...]
        gram = {}
        n = 0
        for i in range(5):
            for j in range(i, 5):
                gram[i, j] = gram[j, i] = total[n]
                n += 1

        def form(a, b):
            whole = None
            for i, left in a.items():
                inner = None
                for j, right in b.items():
                    term = gram[i, j] * right
                    inner = term if inner is None else inner + term
                inner = left * inner
                whole = inner if whole is None else whole + inner
            return whole

        rr0 = gram[0, 0]
        pp = gram[0, 0] + 2.0 * gram[0, 1] + gram[1, 1]
        pbp = gram[0, 2] + gram[0, 3] + gram[1, 2] + gram[1, 3]
        al0 = rr0 / (shift * pp + pbp)
        b, e = -(al0 * shift), -al0
        a = 1.0 + b
        r1 = {0: a, 1: b, 2: e, 3: e}
        rr1 = form(r1, r1)
        be0 = rr1 / rr0
        pa, pb = a + be0, b + be0
        p1 = {0: pa, 1: pb, 2: e, 3: e}
        bp1 = {2: pa, 3: pb, 4: e}
        al1 = rr1 / (shift * form(p1, p1) + form(p1, bp1))
        sc = al1 * shift
        tail = e * (1.0 - sc)
        r2 = {0: a - sc * pa, 1: b - sc * pb, 2: tail - al1 * pa, 3: tail - al1 * pb, 4: -(al1 * e)}
        be1 = form(r2, r2) / rr1
        x0, x1 = al0 + al1 * pa, al0 + al1 * pb
        return r2, (be1 * pa, be1 * pb, be1 * e), (x0, x1, al1 * e)

    def advance(total, first):
        c, gg, xx = two_steps(total)
        t = [st[T0], st[T1], st[T2], first]
        q = [st[G0], st[G1], st[G2], st[G3]]
        h = [None, t[1] + q[1], t[2] + q[2], t[3] + q[3]]
        st[X] = st[X] + xx[0] * t[0] + xx[1] * q[0] + xx[2] * h[1]
        for k, n in enumerate((T0, T1, T2)):
            new = c[2] * t[k + 1] + c[3] * q[k + 1] + c[0] * t[k] + c[1] * q[k]
            st[n] = new if n == T2 else new + c[4] * h[k + 2]
        for k, n in enumerate((G0, G1, G2, G3)):
            new = gg[0] * t[k] + gg[1] * q[k]
            st[n] = new if n == G3 else new + gg[2] * h[k + 1]
        cf[0] = c[4]
        cf[1] = gg[2]

    r0 = deliver_end(1)
    for n in range(8):
        st[n] = jnp.zeros((2, 8, 128), F32)
    st[T0] = r0
    st[T2] = r0

    def outer(o, carry):
        par = lax.rem(o, 2)
        first = operate(0, st[T2], lambda: sum_start(par), lambda: None, False)

        def close_sum():
            total = sum_end(par)

            @pl.when(o == 0)
            def _():
                cs[...] = total[15] * (1.0 / (60.0 * faces_all)) + SHIFT

            @pl.when(o > 0)
            def _():
                advance(total, first)

        second = operate(1, first + st[G3], lambda: sum_middle(par), close_sum, True)

        @pl.when(o == 0)
        def _():
            move = cs[...] - SHIFT
            inside = lax.broadcasted_iota(jnp.int32, (2, 8, 128), 0) * 8 + lax.broadcasted_iota(
                jnp.int32, (2, 8, 128), 1) < 15
            dg[...] = jnp.where(inside, dg[...] - move[None], 0.0)
            t1 = first - move * st[T0]
            st[T1] = t1
            st[T2] = second - move * (first + t1)

        @pl.when(o > 0)
        def _():
            st[T2] = st[T2] + cf[0] * second
            st[G3] = st[G3] + cf[1] * second

        return carry

    lax.fori_loop(0, 4, outer, 0)
    sum_start(0)
    sum_middle(0)
    r2, gg, xx = two_steps(sum_end(0))
    t, q = [st[T0], st[T1], st[T2]], [st[G0], st[G1], st[G2]]
    x = st[X] + xx[0] * t[0] + xx[1] * q[0] + xx[2] * (t[1] + q[1])
    r = (r2[4] * (t[2] + q[2]) + r2[2] * t[1] + r2[3] * q[1] + r2[0] * t[0] + r2[1] * q[0])
    sol_ref[...] = x.reshape(16, 128)[0:15]
    res_ref[...] = r.reshape(16, 128)[0:15]


def solution(mesh):
    n_dom, n_grp = mesh.shape["dom"], mesh.shape["grp"]

    def on_device(element_faces, interior_load, inverses, lift_operator, face_area, columns, blocks, diagonal):
        args = (element_faces, interior_load, inverses, lift_operator, face_area, columns, blocks, diagonal)
        order = (0, 1, 2, 3, 4, 5, 6, 7)
        slots, zs = columns.shape[0], n_dom // 8
        dma, vmem = pltpu.SemaphoreType.DMA, pltpu.VMEM
        faces_all = float(diagonal.shape[1] * n_dom)

        def body(*refs):
            kernel(n_dom, n_grp, faces_all, *refs)

        found = pl.pallas_call(
            body,
            out_shape=(jax.ShapeDtypeStruct(diagonal.shape, F32),) * 2,
            in_specs=[pl.BlockSpec(memory_space=pl.ANY)] * 8,
            out_specs=(pl.BlockSpec(memory_space=pltpu.VMEM),) * 2,
            scratch_shapes=[vmem(args[i].shape, args[i].dtype) for i in order]
            + [
                vmem((slots, n_grp, 15, 2, 8, 128), F32),
                vmem((2, 8, 128), F32),
                vmem((slots - 1, 8, 128), jnp.int32),
                vmem((slots - 1, 8, 128), jnp.int32),
                vmem((slots - 1, 3, 8, 128), jnp.int32),
                vmem((60, 384), F32),
                vmem((2, 3, 4, 2, 8, 128), F32),
                vmem((3, 4, 2, 8, 128), F32),
                vmem((2, 3, 4, 2, 8, 128), F32),
                vmem((slots, n_grp, 2, 8, 128), F32),
                vmem((2, 32, 1, 128), F32),
                vmem((2, zs, 1, 128), F32),
                vmem((8, 2, 8, 128), F32),
                vmem((8, 128), F32),
                vmem((2, 8, 128), F32),
                dma((8,)), dma((3, 4)), dma((2, 3, 4)), dma((3, 4)), dma((2, 3, 4)),
                dma((16,)), dma((2, 32)), dma((2, zs)), dma((2, zs)),
            ],
            compiler_params=pltpu.CompilerParams(
                collective_id=0, has_side_effects=True, vmem_limit_bytes=40 * 1024 * 1024),
            name="cg",
        )(*[pltpu.with_memory_space_constraint(a, pltpu.HBM) for a in args])

        return found

    return jax.shard_map(
        on_device,
        mesh=mesh,
        in_specs=(
            P(None, "dom"), P(None, "dom"), P("grp", None, "dom"), P("grp", None), P(None, "dom"),
            P(None, "dom"), P(None, "grp", None, "dom"), P("grp", "dom"),
        ),
        out_specs=(P("grp", "dom"), P("grp", "dom")),
        check_vma=False,
    )
```

```python
import jax
import jax.numpy as jnp
from jax import lax
from jax.experimental import pallas as pl
from jax.experimental.pallas import tpu as pltpu
from jax.sharding import PartitionSpec as P

MESH = pl.DeviceIdType.MESH
F32 = jnp.float32
SHIFT = 1.16
FAR_FIRST = (2, 1, 3, 0)
A_ORDER = (10, 9, 11, 6, 14, 5, 7, 13, 15, 8, 2, 4, 12, 1, 3)
OUT, IN, OWN = 1, -1, 0
LINKS = [(OUT, h) for h in FAR_FIRST] + [(IN, h) for h in FAR_FIRST] + [(OWN, 2), (OWN, 1), (OWN, 3)]


def wide(row, rows):
    return jnp.broadcast_to(row, (rows, row.shape[-1]))


def pick(value, lanes):
    return jnp.take_along_axis(value, lanes, axis=1, mode="promise_in_bounds")


def kernel(
    n_dom, n_grp, faces_all,
    faces_h, load_h, inv_h, lift_h, area_h, cols_h, raw_h, diag_h,
    sol_ref, res_ref,
    faces, load, inv, lift, area, cols, raw, diag,
    blk, dg, lanes_of, part_of, back, slab, vrecv, tsend, trecv, hold, ra, rb, st, cs, cf,
    in_sem, vs_sem, vr_sem, ts_sem, tr_sem, as_sem, ar_sem, bs_sem, br_sem, ready,
):
    d, g = lax.axis_index("dom"), lax.axis_index("grp")
    core = lax.rem(d, 2)
    y = lax.rem(d // 2, 4)
    z = d // 8
    zs = n_dom // 8
    slots = blk.shape[0]

    loads = [
        pltpu.make_async_copy(a, b, in_sem.at[i])
        for i, (a, b) in enumerate(
            [(inv_h, inv), (load_h, load), (lift_h, lift), (area_h, area), (faces_h, faces),
             (cols_h, cols), (diag_h, diag), (raw_h, raw)]
        )
    ]
    away = 2 * core - 1

    def link(s, h):
        s = s * away
        return lax.rem(d + s + n_dom, n_dom), lax.rem(g + h, n_grp)

    def peer_a(dy, dx, c):
        return (z * 4 + lax.rem(y + dy, 4)) * 2 + c, lax.rem(g + dx, 4)

    def peer_b(dz, c):
        return (lax.rem(z + dz, zs) * 4 + y) * 2 + c, g

    group_a = [(a, b) for a in range(4) for b in range(4)]
    b_order = sorted(range(1, zs), key=lambda n: -min(n, zs - n))
    ends_low, ends_high = (3 - g) // 3, g // 3
    far = [2 + ends_low, 3 - ends_low - 2 * ends_high]
    far = far + [6 - far[0] - far[1], 0]
    near = far[::-1]
    bar = pltpu.get_barrier_semaphore()

    def greet(who):
        pl.semaphore_signal(bar, inc=1, device_id=who, device_id_type=MESH)

    edge = (n_dom - 1 - d) // (n_dom - 1) + d // (n_dom - 1)

    def inside(run):
        pl.when(edge == 0)(run)

    @pl.when(edge == 1)
    def _():
        vrecv[...] = jnp.zeros(vrecv.shape, F32)
        trecv[...] = jnp.zeros(trecv.shape, F32)

    @inside
    def _():
        for h in far:
            greet(link(OUT, h))


    @pl.when(core == 1)
    def _():
        for n in A_ORDER:
            if n >= 4:
                greet(peer_a(*group_a[n], 0))
                greet(peer_a(*group_a[n], 1))

    for s, h in LINKS[4:]:
        greet(link(s, h))
    for c in loads:
        c.start()
    for n in range(1, zs):

        @pl.when(z + n < zs)
        def _():
            greet(peer_b(n, 1))

            @pl.when(core == 1)
            def _():
                greet(peer_b(n, 0))

    greetings = len(LINKS) - 4 * edge + 12 + z * (1 + core)

    def t_copy(par, s, h):
        peer = link(s, h)
        s = s * away
        return pltpu.make_async_remote_copy(
            tsend.at[s + 1, peer[1]], trecv.at[par, s + 1, g], ts_sem.at[s + 1, h],
            tr_sem.at[par, s + 1, g], device_id=peer, device_id_type=MESH)

    def t_from(par, s, h):
        src, peer = lax.rem(g + n_grp - h, n_grp), link(s, h)
        s = -s * away
        return pltpu.make_async_remote_copy(
            tsend.at[s + 1, g], trecv.at[par, s + 1, src], ts_sem.at[s + 1, h],
            tr_sem.at[par, s + 1, src], device_id=peer, device_id_type=MESH)

    def v_copy(par, s, h):
        peer = link(s, h)
        s = s * away
        return pltpu.make_async_remote_copy(
            vrecv.at[par, 1, g], vrecv.at[par, 1 - s, g], vs_sem.at[s + 1, h],
            vr_sem.at[par, 1 - s, g], device_id=peer, device_id_type=MESH)

    def v_from(par, s, h):
        src, peer = lax.rem(g + n_grp - h, n_grp), link(s, h)
        s = s * away
        return pltpu.make_async_remote_copy(
            vrecv.at[par, 1, g], vrecv.at[par, 1 + s, src], vs_sem.at[s + 1, h],
            vr_sem.at[par, 1 + s, src], device_id=peer, device_id_type=MESH)

    def deliver_start(par):
        trecv[par, 1, g] = tsend[1, g]

        @inside
        def _():
            for h in far:
                t_copy(par, OUT, h).start()

        for s, h in LINKS[4:]:
            t_copy(par, s, h).start()

    def deliver_end(par):
        @inside
        def _():
            for s, h in LINKS[:4]:
                t_from(par, s, h).wait_recv()
                t_copy(par, s, h).wait_send()

        for s, h in LINKS[4:]:
            t_from(par, s, h).wait_recv()
        total = trecv[par, 0, 0]
        for s in range(3):
            for k in range(4):
                if (s, k) != (0, 0):
                    total = total + trecv[par, s, k]
        for s, h in LINKS[4:]:
            t_copy(par, s, h).wait_send()
        return total

    for c in loads[:5]:
        c.wait()
    interior = jnp.sum(inv[...].astype(F32) * load[...].astype(F32)[None], axis=1)
    base = (d - 1) * 128
    ends = lax.broadcasted_iota(jnp.int32, (384, 128), 0)
    out = jnp.zeros((60, 384), F32)
    for k in range(4):
        lifted = lax.dot_general(
            lift[:, 60 * k : 60 * k + 60], interior, (((0,), (0,)), ((), ())),
            precision=lax.Precision.HIGHEST, preferred_element_type=F32)
        rest = -(lifted * area[k : k + 1])
        hit = (wide(faces[k : k + 1] - base, 384) == ends).astype(F32).astype(jnp.bfloat16)
        for _ in range(3):
            part = rest.astype(jnp.bfloat16)
            rest = rest - part.astype(F32)
            out = out + lax.dot_general(
                part, hit, (((1,), (1,)), ((), ())), preferred_element_type=F32)
    slab[...] = out
    tsend[...] = jnp.zeros(tsend.shape, F32)
    for s in range(3):
        for k in range(4):
            tsend[s, k, 0] = slab[15 * k : 15 * k + 8, 128 * s : 128 * s + 128]
            tsend[s, k, 1, 0:7] = slab[15 * k + 8 : 15 * k + 15, 128 * s : 128 * s + 128]
    pl.semaphore_wait(bar, greetings)
    deliver_start(1)
    for n in range(1, zs):

        @pl.when(z - n >= 0)
        def _():
            who = (((z - n) * 4 + y) * 2 + 1, g)
            pl.semaphore_signal(ready, inc=1, device_id=who, device_id_type=MESH)


    for c in loads[5:]:
        c.wait()
    dg[...] = jnp.zeros(dg.shape, F32)
    dg[0] = diag[0:8] - SHIFT
    dg[1, 0:7] = diag[8:15] - SHIFT

    blk[...] = jnp.zeros(blk.shape, F32)

    def respace(n, carry):
        s, i = n // 15, lax.rem(n, 15)
        for k in range(4):
            blk[s, k, i, 0] = raw[s, i, 15 * k : 15 * k + 8]
            blk[s, k, i, 1, 0:7] = raw[s, i, 15 * k + 8 : 15 * k + 15]
        return carry

    lax.fori_loop(0, slots * 15, respace, 0)
    numbers = lax.broadcasted_iota(jnp.int32, (8, 128), 1).astype(F32) + 1.0
    numbers = numbers.astype(jnp.bfloat16)
    for s in range(1, slots):
        row = cols[s : s + 1]
        there = jnp.where(row >= 0, row - base, -1)
        lanes_of[s - 1] = wide(there & 127, 8)
        part_of[s - 1] = wide(there >> 7, 8)
        hit = (wide(there, 384) == ends).astype(F32).astype(jnp.bfloat16)
        found = lax.dot_general(
            numbers, hit, (((1,), (1,)), ((), ())), preferred_element_type=F32)
        found = found.astype(jnp.int32) - 1
        for k in range(3):
            back[s - 1, k] = found[:, 128 * k : 128 * k + 128]

    def twice(value):
        return jnp.broadcast_to(value[None], (2, 8, 128)).reshape(16, 128)

    def scatter(s, turned, p):
        lane = back[s - 1, p]
        moved = pick(turned.reshape(16, 128), twice(lane & 127))
        return jnp.where(twice(lane) >= 0, moved, 0.0).reshape(2, 8, 128)

    def operate(par, v, during, late, early):
        vrecv[par, 1, g] = v

        @inside
        def _():
            for h in far[:2]:
                v_copy(par, OUT, h).start()

        rows = v.reshape(16, 128)
        vb = jnp.concatenate([wide(rows[i : i + 1], 8)[None] for i in range(15)], axis=0)
        for h in far:
            k = lax.rem(g + h, n_grp)
            out = None
            for s in range(slots):
                turned = jnp.sum(blk[s, k] * vb[:, None], axis=0)
                hold[s, k] = turned
                if s:
                    moved = scatter(s, turned, 1 + away)
                    out = moved if out is None else out + moved
            tsend[1 + away, k] = out

            @inside
            def _():
                t_copy(par, OUT, h).start()
                if h is far[1]:
                    v_copy(par, OUT, far[2]).start()
                if h is far[2]:
                    v_copy(par, OUT, far[3]).start()

        if early:
            during()
        for h in far:
            k = lax.rem(g + h, n_grp)
            own, inner = hold[0, k], None
            for s in range(1, slots):
                turned = hold[s, k]
                own = own + scatter(s, turned, 1)
                moved = scatter(s, turned, 1 - away)
                inner = moved if inner is None else inner + moved
            tsend[1, k] = own
            tsend[1 - away, k] = inner
            if h is not far[3]:
                v_copy(par, OWN, h).start()
                t_copy(par, OWN, h).start()
            else:
                trecv[par, 1, g] = own
            v_copy(par, IN, h).start()
            t_copy(par, IN, h).start()
        if not early:
            during()
        acc = jnp.zeros((15, 8, 128), F32)
        for h in near:
            k = lax.rem(g + h, n_grp)
            back_h = lax.rem(n_grp - h, n_grp)
            for s in (OWN, IN):
                if s != OWN or h is not near[0]:
                    v_from(par, s, back_h).wait_recv()

            @inside
            def _():
                v_from(par, OUT, back_h).wait_recv()

            parts = [vrecv[par, p, k].reshape(16, 128) for p in range(3)]
            for s in range(slots):
                if s == 0:
                    taken = parts[1]
                else:
                    lane, part = twice(lanes_of[s - 1]), twice(part_of[s - 1])
                    taken = jnp.zeros((16, 128), F32)
                    for p in range(3):
                        taken = jnp.where(part == p, pick(parts[p], lane), taken)
                acc = acc + jnp.sum(blk[s, k] * taken.reshape(1, 2, 8, 128), axis=1)
        rows = jnp.concatenate([jnp.sum(acc, axis=1), jnp.zeros((1, 128), F32)], axis=0)
        result = dg[...] * v + rows.reshape(2, 8, 128)
        late()
        for s, h in LINKS[4:]:
            t_copy(par, s, h).wait_send()
            v_copy(par, s, h).wait_send()

        @inside
        def _():
            for s, h in LINKS[:4]:
                t_copy(par, s, h).wait_send()
                v_copy(par, s, h).wait_send()

        result = result + trecv[par, 1, g]
        for h in near:
            k = lax.rem(g + h, n_grp)
            for s in (OWN, IN):
                if s != OWN or h is not near[0]:
                    t_from(par, s, lax.rem(n_grp - h, n_grp)).wait_recv()
                    result = result + trecv[par, 1 - s * away, k]

        @inside
        def _():
            for h in near:
                t_from(par, OUT, lax.rem(n_grp - h, n_grp)).wait_recv()

        for h in near:
            result = result + trecv[par, 1 - away, lax.rem(g + h, n_grp)]
        return result

    me_a = (y * 4 + g) * 2 + core

    def a_copy(par, n):
        dy, dx = group_a[n]
        return pltpu.make_async_remote_copy(
            ra.at[par, me_a], ra.at[par, me_a], as_sem.at[n], ar_sem.at[par, me_a],
            device_id=peer_a(dy, dx, 1), device_id_type=MESH)

    def a_from(par, n, c):
        dy, dx = group_a[n]
        src = (lax.rem(y + 4 - dy, 4) * 4 + lax.rem(g + 4 - dx, 4)) * 2 + c
        return pltpu.make_async_remote_copy(
            ra.at[par, me_a], ra.at[par, src], as_sem.at[n], ar_sem.at[par, src],
            device_id=peer_a(dy, dx, 1), device_id_type=MESH)

    def b_copy(par, dz, c):
        return pltpu.make_async_remote_copy(
            rb.at[par, z], rb.at[par, z], bs_sem.at[c, dz], br_sem.at[par, z],
            device_id=peer_b(dz, c), device_id_type=MESH)

    def b_from(par, dz):
        src = lax.rem(z + zs - dz, zs)
        return pltpu.make_async_remote_copy(
            rb.at[par, z], rb.at[par, src], bs_sem.at[0, dz], br_sem.at[par, src],
            device_id=peer_b(dz, 1 - core), device_id_type=MESH)

    T0, T1, T2, G0, G1, G2, G3, X = range(8)

    def sum_start(par):
        basis = [st[T0], st[G0], st[T1], st[G1], st[T2] + st[G2]]
        items = [basis[i] * basis[j] for i in range(5) for j in range(i, 5)] + [dg[...]]
        both = jnp.concatenate([(a[0] + a[1])[None] for a in items], axis=0)
        flat = jnp.sum(jnp.sum(both, axis=1), axis=1, keepdims=True)
        keep = lax.broadcasted_iota(jnp.int32, (16, 128), 0) == lax.broadcasted_iota(
            jnp.int32, (16, 128), 1)
        row = jnp.sum(jnp.where(keep, jnp.broadcast_to(flat, (16, 128)), 0.0), axis=0, keepdims=True)
        ra[par, me_a] = row
        for n in A_ORDER:
            a_copy(par, n).start()

        @pl.when(core == 0)
        def _():
            a_copy(par, 0).start()

    def sum_middle(par):
        @pl.when(core == 1)
        def _():
            for n in range(16):
                a_from(par, n, 0).wait_recv()
                if n:
                    a_from(par, n, 1).wait_recv()
            rb[par, z] = jnp.sum(ra[par], axis=0)
            for n in b_order:
                b_copy(par, n, 0).start()
                b_copy(par, n, 1).start()
            b_copy(par, 0, 0).start()

        for n in range(1, 16):
            a_copy(par, n).wait_send()

        @pl.when(core == 0)
        def _():
            a_copy(par, 0).wait_send()

    def sum_end(par):
        for n in range(1, zs):
            b_from(par, n).wait_recv()

        @pl.when(core == 0)
        def _():
            b_from(par, 0).wait_recv()

        total = jnp.sum(rb[par], axis=0)

        @pl.when(core == 1)
        def _():
            for n in range(1, zs):
                b_copy(par, n, 0).wait_send()
                b_copy(par, n, 1).wait_send()
            b_copy(par, 0, 0).wait_send()

        return [jnp.broadcast_to(total[:, n : n + 1], (8, 128)) for n in range(16)]

    def two_steps(total):
        shift = cs[...]
        gram = {}
        n = 0
        for i in range(5):
            for j in range(i, 5):
                gram[i, j] = gram[j, i] = total[n]
                n += 1

        def form(a, b):
            whole = None
            for i, left in a.items():
                inner = None
                for j, right in b.items():
                    term = gram[i, j] * right
                    inner = term if inner is None else inner + term
                inner = left * inner
                whole = inner if whole is None else whole + inner
            return whole

        rr0 = gram[0, 0]
        pp = gram[0, 0] + 2.0 * gram[0, 1] + gram[1, 1]
        pbp = gram[0, 2] + gram[0, 3] + gram[1, 2] + gram[1, 3]
        al0 = rr0 / (shift * pp + pbp)
        b, e = -(al0 * shift), -al0
        a = 1.0 + b
        r1 = {0: a, 1: b, 2: e, 3: e}
        rr1 = form(r1, r1)
        be0 = rr1 / rr0
        pa, pb = a + be0, b + be0
        p1 = {0: pa, 1: pb, 2: e, 3: e}
        bp1 = {2: pa, 3: pb, 4: e}
        al1 = rr1 / (shift * form(p1, p1) + form(p1, bp1))
        sc = al1 * shift
        tail = e * (1.0 - sc)
        r2 = {0: a - sc * pa, 1: b - sc * pb, 2: tail - al1 * pa, 3: tail - al1 * pb, 4: -(al1 * e)}
        be1 = form(r2, r2) / rr1
        x0, x1 = al0 + al1 * pa, al0 + al1 * pb
        return r2, (be1 * pa, be1 * pb, be1 * e), (x0, x1, al1 * e)

    def advance(total, first):
        c, gg, xx = two_steps(total)
        t = [st[T0], st[T1], st[T2], first]
        q = [st[G0], st[G1], st[G2], st[G3]]
        h = [None, t[1] + q[1], t[2] + q[2], t[3] + q[3]]
        st[X] = st[X] + xx[0] * t[0] + xx[1] * q[0] + xx[2] * h[1]
        for k, n in enumerate((T0, T1, T2)):
            new = c[2] * t[k + 1] + c[3] * q[k + 1] + c[0] * t[k] + c[1] * q[k]
            st[n] = new if n == T2 else new + c[4] * h[k + 2]
        for k, n in enumerate((G0, G1, G2, G3)):
            new = gg[0] * t[k] + gg[1] * q[k]
            st[n] = new if n == G3 else new + gg[2] * h[k + 1]
        cf[0] = c[4]
        cf[1] = gg[2]

    r0 = deliver_end(1)
    for n in range(8):
        st[n] = jnp.zeros((2, 8, 128), F32)
    st[T0] = r0
    st[T2] = r0

    def outer(o, carry):
        par = lax.rem(o, 2)

        def middle():
            @pl.when((o == 0) & (core == 1) & (z < zs - 1))
            def _():
                pl.semaphore_wait(ready, 2 * (zs - 1 - z))

            sum_middle(par)

        first = operate(0, st[T2], lambda: sum_start(par), lambda: None, False)

        def close_sum():
            total = sum_end(par)

            @pl.when(o == 0)
            def _():
                cs[...] = total[15] * (1.0 / (60.0 * faces_all)) + SHIFT

            @pl.when(o > 0)
            def _():
                advance(total, first)

        second = operate(1, first + st[G3], middle, close_sum, True)

        @pl.when(o == 0)
        def _():
            move = cs[...] - SHIFT
            inside = lax.broadcasted_iota(jnp.int32, (2, 8, 128), 0) * 8 + lax.broadcasted_iota(
                jnp.int32, (2, 8, 128), 1) < 15
            dg[...] = jnp.where(inside, dg[...] - move[None], 0.0)
            t1 = first - move * st[T0]
            st[T1] = t1
            st[T2] = second - move * (first + t1)

        @pl.when(o > 0)
        def _():
            st[T2] = st[T2] + cf[0] * second
            st[G3] = st[G3] + cf[1] * second

        return carry

    lax.fori_loop(0, 4, outer, 0)
    sum_start(0)
    sum_middle(0)
    r2, gg, xx = two_steps(sum_end(0))
    t, q = [st[T0], st[T1], st[T2]], [st[G0], st[G1], st[G2]]
    x = st[X] + xx[0] * t[0] + xx[1] * q[0] + xx[2] * (t[1] + q[1])
    r = (r2[4] * (t[2] + q[2]) + r2[2] * t[1] + r2[3] * q[1] + r2[0] * t[0] + r2[1] * q[0])
    sol_ref[...] = x.reshape(16, 128)[0:15]
    res_ref[...] = r.reshape(16, 128)[0:15]


def solution(mesh):
    n_dom, n_grp = mesh.shape["dom"], mesh.shape["grp"]

    def on_device(element_faces, interior_load, inverses, lift_operator, face_area, columns, blocks, diagonal):
        args = (element_faces, interior_load, inverses, lift_operator, face_area, columns, blocks, diagonal)
        slots, zs = columns.shape[0], n_dom // 8
        dma, vmem = pltpu.SemaphoreType.DMA, pltpu.VMEM
        faces_all = float(diagonal.shape[1] * n_dom)

        def body(*refs):
            kernel(n_dom, n_grp, faces_all, *refs)

        found = pl.pallas_call(
            body,
            out_shape=(jax.ShapeDtypeStruct(diagonal.shape, F32),) * 2,
            in_specs=[pl.BlockSpec(memory_space=pl.ANY)] * 8,
            out_specs=(pl.BlockSpec(memory_space=pltpu.VMEM),) * 2,
            scratch_shapes=[vmem(a.shape, a.dtype) for a in args]
            + [
                vmem((slots, n_grp, 15, 2, 8, 128), F32),
                vmem((2, 8, 128), F32),
                vmem((slots - 1, 8, 128), jnp.int32),
                vmem((slots - 1, 8, 128), jnp.int32),
                vmem((slots - 1, 3, 8, 128), jnp.int32),
                vmem((60, 384), F32),
                vmem((2, 3, 4, 2, 8, 128), F32),
                vmem((3, 4, 2, 8, 128), F32),
                vmem((2, 3, 4, 2, 8, 128), F32),
                vmem((slots, n_grp, 2, 8, 128), F32),
                vmem((2, 32, 1, 128), F32),
                vmem((2, zs, 1, 128), F32),
                vmem((8, 2, 8, 128), F32),
                vmem((8, 128), F32),
                vmem((2, 8, 128), F32),
                dma((8,)), dma((3, 4)), dma((2, 3, 4)), dma((3, 4)), dma((2, 3, 4)),
                dma((16,)), dma((2, 32)), dma((2, zs)), dma((2, zs)),
                pltpu.SemaphoreType.REGULAR,
            ],
            compiler_params=pltpu.CompilerParams(
                collective_id=0, has_side_effects=True, vmem_limit_bytes=40 * 1024 * 1024),
            name="cg",
        )(*[pltpu.with_memory_space_constraint(a, pltpu.HBM) for a in args])

        return found

    return jax.shard_map(
        on_device,
        mesh=mesh,
        in_specs=(
            P(None, "dom"), P(None, "dom"), P("grp", None, "dom"), P("grp", None), P(None, "dom"),
            P(None, "dom"), P(None, "grp", None, "dom"), P("grp", "dom"),
        ),
        out_specs=(P("grp", "dom"), P("grp", "dom")),
        check_vma=False,
    )
```

```python
import jax
import jax.numpy as jnp
from jax import lax
from jax.experimental import pallas as pl
from jax.experimental.pallas import tpu as pltpu
from jax.sharding import PartitionSpec as P

MESH = pl.DeviceIdType.MESH
F32 = jnp.float32
SHIFT = 1.16
FAR_FIRST = (2, 1, 3, 0)
A_ORDER = (10, 9, 11, 6, 14, 5, 7, 13, 15, 8, 2, 4, 12, 1, 3)
OUT, IN, OWN = 1, -1, 0
LINKS = [(OUT, h) for h in FAR_FIRST] + [(IN, h) for h in FAR_FIRST] + [(OWN, 2), (OWN, 1), (OWN, 3)]


def wide(row, rows):
    return jnp.broadcast_to(row, (rows, row.shape[-1]))


def pick(value, lanes):
    return jnp.take_along_axis(value, lanes, axis=1, mode="promise_in_bounds")


def kernel(
    n_dom, n_grp, faces_all,
    faces_h, load_h, inv_h, lift_h, area_h, cols_h, raw_h, diag_h,
    sol_ref, res_ref,
    faces, load, inv, lift, area, cols, raw, diag,
    blk, dg, lanes_of, part_of, back, slab, vrecv, tsend, trecv, hold, ra, rb, st, cs, cf,
    in_sem, vs_sem, vr_sem, ts_sem, tr_sem, as_sem, ar_sem, bs_sem, br_sem, ready,
):
    d, g = lax.axis_index("dom"), lax.axis_index("grp")
    core = lax.rem(d, 2)
    y = lax.rem(d // 2, 4)
    z = d // 8
    zs = n_dom // 8
    slots = blk.shape[0]

    loads = [
        pltpu.make_async_copy(a, b, in_sem.at[i])
        for i, (a, b) in enumerate(
            [(inv_h, inv), (load_h, load), (lift_h, lift), (area_h, area), (faces_h, faces),
             (cols_h, cols), (diag_h, diag), (raw_h, raw)]
        )
    ]
    away = 2 * core - 1

    def link(s, h):
        s = s * away
        return lax.rem(d + s + n_dom, n_dom), lax.rem(g + h, n_grp)

    def peer_a(dy, dx, c):
        return (z * 4 + lax.rem(y + dy, 4)) * 2 + c, lax.rem(g + dx, 4)

    def peer_b(dz, c):
        return (lax.rem(z + dz, zs) * 4 + y) * 2 + c, g

    group_a = [(a, b) for a in range(4) for b in range(4)]
    b_order = sorted(range(1, zs), key=lambda n: -min(n, zs - n))
    ends_low, ends_high = (3 - g) // 3, g // 3
    far = [2 + ends_low, 3 - ends_low - 2 * ends_high]
    far = far + [6 - far[0] - far[1], 0]
    near = far[::-1]
    bar = pltpu.get_barrier_semaphore()

    def greet(who):
        pl.semaphore_signal(bar, inc=1, device_id=who, device_id_type=MESH)

    edge = (n_dom - 1 - d) // (n_dom - 1) + d // (n_dom - 1)

    def inside(run):
        pl.when(edge == 0)(run)

    @pl.when(edge == 1)
    def _():
        vrecv[...] = jnp.zeros(vrecv.shape, F32)
        trecv[...] = jnp.zeros(trecv.shape, F32)

    @inside
    def _():
        for h in far:
            greet(link(OUT, h))


    @pl.when(core == 1)
    def _():
        for n in A_ORDER:
            if n >= 4:
                greet(peer_a(*group_a[n], 0))
                greet(peer_a(*group_a[n], 1))

    for s, h in LINKS[4:]:
        greet(link(s, h))
    for c in loads:
        c.start()
    for n in range(1, zs):

        @pl.when(z + n < zs)
        def _():
            greet(peer_b(n, 1))

            @pl.when(core == 1)
            def _():
                greet(peer_b(n, 0))

    greetings = len(LINKS) - 4 * edge + 12 + z * (1 + core)

    def t_copy(par, s, h):
        peer = link(s, h)
        s = s * away
        return pltpu.make_async_remote_copy(
            tsend.at[s + 1, peer[1]], trecv.at[par, s + 1, g], ts_sem.at[s + 1, h],
            tr_sem.at[par, s + 1, g], device_id=peer, device_id_type=MESH)

    def t_from(par, s, h):
        src, peer = lax.rem(g + n_grp - h, n_grp), link(s, h)
        s = -s * away
        return pltpu.make_async_remote_copy(
            tsend.at[s + 1, g], trecv.at[par, s + 1, src], ts_sem.at[s + 1, h],
            tr_sem.at[par, s + 1, src], device_id=peer, device_id_type=MESH)

    def v_copy(par, s, h):
        peer = link(s, h)
        s = s * away
        return pltpu.make_async_remote_copy(
            vrecv.at[par, 1, g], vrecv.at[par, 1 - s, g], vs_sem.at[s + 1, h],
            vr_sem.at[par, 1 - s, g], device_id=peer, device_id_type=MESH)

    def v_from(par, s, h):
        src, peer = lax.rem(g + n_grp - h, n_grp), link(s, h)
        s = s * away
        return pltpu.make_async_remote_copy(
            vrecv.at[par, 1, g], vrecv.at[par, 1 + s, src], vs_sem.at[s + 1, h],
            vr_sem.at[par, 1 + s, src], device_id=peer, device_id_type=MESH)

    def deliver_start(par):
        trecv[par, 1, g] = tsend[1, g]

        @inside
        def _():
            for h in far:
                t_copy(par, OUT, h).start()

        for s, h in LINKS[4:]:
            t_copy(par, s, h).start()

    def deliver_end(par):
        @inside
        def _():
            for s, h in LINKS[:4]:
                t_from(par, s, h).wait_recv()
                t_copy(par, s, h).wait_send()

        for s, h in LINKS[4:]:
            t_from(par, s, h).wait_recv()
        total = trecv[par, 0, 0]
        for s in range(3):
            for k in range(4):
                if (s, k) != (0, 0):
                    total = total + trecv[par, s, k]
        for s, h in LINKS[4:]:
            t_copy(par, s, h).wait_send()
        return total

    for c in loads[:5]:
        c.wait()
    interior = jnp.sum(inv[...].astype(F32) * load[...].astype(F32)[None], axis=1)
    base = (d - 1) * 128
    ends = lax.broadcasted_iota(jnp.int32, (384, 128), 0)
    out = jnp.zeros((60, 384), F32)
    for k in range(4):
        lifted = lax.dot_general(
            lift[:, 60 * k : 60 * k + 60], interior, (((0,), (0,)), ((), ())),
            precision=lax.Precision.HIGHEST, preferred_element_type=F32)
        rest = -(lifted * area[k : k + 1])
        hit = (wide(faces[k : k + 1] - base, 384) == ends).astype(F32).astype(jnp.bfloat16)
        for _ in range(3):
            part = rest.astype(jnp.bfloat16)
            rest = rest - part.astype(F32)
            out = out + lax.dot_general(
                part, hit, (((1,), (1,)), ((), ())), preferred_element_type=F32)
    slab[...] = out
    tsend[...] = jnp.zeros(tsend.shape, F32)
    for s in range(3):
        for k in range(4):
            tsend[s, k, 0] = slab[15 * k : 15 * k + 8, 128 * s : 128 * s + 128]
            tsend[s, k, 1, 0:7] = slab[15 * k + 8 : 15 * k + 15, 128 * s : 128 * s + 128]
    for c in loads[5:7]:
        c.wait()
    dg[...] = jnp.zeros(dg.shape, F32)
    dg[0] = diag[0:8] - SHIFT
    dg[1, 0:7] = diag[8:15] - SHIFT

    numbers = lax.broadcasted_iota(jnp.int32, (8, 128), 1).astype(F32) + 1.0
    numbers = numbers.astype(jnp.bfloat16)
    for s in range(1, slots):
        row = cols[s : s + 1]
        there = jnp.where(row >= 0, row - base, -1)
        lanes_of[s - 1] = wide(there & 127, 8)
        part_of[s - 1] = wide(there >> 7, 8)
        hit = (wide(there, 384) == ends).astype(F32).astype(jnp.bfloat16)
        found = lax.dot_general(
            numbers, hit, (((1,), (1,)), ((), ())), preferred_element_type=F32)
        found = found.astype(jnp.int32) - 1
        for k in range(3):
            back[s - 1, k] = found[:, 128 * k : 128 * k + 128]

    for n in range(8):
        st[n] = jnp.zeros((2, 8, 128), F32)
    pl.semaphore_wait(bar, greetings)
    deliver_start(1)
    for n in range(1, zs):

        @pl.when(z - n >= 0)
        def _():
            who = (((z - n) * 4 + y) * 2 + 1, g)
            pl.semaphore_signal(ready, inc=1, device_id=who, device_id_type=MESH)


    loads[7].wait()
    blk[...] = jnp.zeros(blk.shape, F32)

    def respace(n, carry):
        s, i = n // 15, lax.rem(n, 15)
        for k in range(4):
            blk[s, k, i, 0] = raw[s, i, 15 * k : 15 * k + 8]
            blk[s, k, i, 1, 0:7] = raw[s, i, 15 * k + 8 : 15 * k + 15]
        return carry

    lax.fori_loop(0, slots * 15, respace, 0)
    def twice(value):
        return jnp.broadcast_to(value[None], (2, 8, 128)).reshape(16, 128)

    def scatter(s, turned, p):
        lane = back[s - 1, p]
        moved = pick(turned.reshape(16, 128), twice(lane & 127))
        return jnp.where(twice(lane) >= 0, moved, 0.0).reshape(2, 8, 128)

    def operate(par, v, during, late, early):
        vrecv[par, 1, g] = v

        @inside
        def _():
            for h in far[:2]:
                v_copy(par, OUT, h).start()

        rows = v.reshape(16, 128)
        vb = jnp.concatenate([wide(rows[i : i + 1], 8)[None] for i in range(15)], axis=0)
        for h in far:
            k = lax.rem(g + h, n_grp)
            out = None
            for s in range(slots):
                turned = jnp.sum(blk[s, k] * vb[:, None], axis=0)
                hold[s, k] = turned
                if s:
                    moved = scatter(s, turned, 1 + away)
                    out = moved if out is None else out + moved
            tsend[1 + away, k] = out

            @inside
            def _():
                t_copy(par, OUT, h).start()
                if h is far[1]:
                    v_copy(par, OUT, far[2]).start()
                if h is far[2]:
                    v_copy(par, OUT, far[3]).start()

        if early:
            during()
        for h in far:
            k = lax.rem(g + h, n_grp)
            own, inner = hold[0, k], None
            for s in range(1, slots):
                turned = hold[s, k]
                own = own + scatter(s, turned, 1)
                moved = scatter(s, turned, 1 - away)
                inner = moved if inner is None else inner + moved
            tsend[1, k] = own
            tsend[1 - away, k] = inner
            if h is not far[3]:
                v_copy(par, OWN, h).start()
                t_copy(par, OWN, h).start()
            else:
                trecv[par, 1, g] = own
            v_copy(par, IN, h).start()
            t_copy(par, IN, h).start()
        if not early:
            during()
        acc = jnp.zeros((15, 8, 128), F32)
        for h in near:
            k = lax.rem(g + h, n_grp)
            back_h = lax.rem(n_grp - h, n_grp)
            for s in (OWN, IN):
                if s != OWN or h is not near[0]:
                    v_from(par, s, back_h).wait_recv()

            @inside
            def _():
                v_from(par, OUT, back_h).wait_recv()

            parts = [vrecv[par, p, k].reshape(16, 128) for p in range(3)]
            for s in range(slots):
                if s == 0:
                    taken = parts[1]
                else:
                    lane, part = twice(lanes_of[s - 1]), twice(part_of[s - 1])
                    taken = jnp.zeros((16, 128), F32)
                    for p in range(3):
                        taken = jnp.where(part == p, pick(parts[p], lane), taken)
                acc = acc + jnp.sum(blk[s, k] * taken.reshape(1, 2, 8, 128), axis=1)
        rows = jnp.concatenate([jnp.sum(acc, axis=1), jnp.zeros((1, 128), F32)], axis=0)
        result = dg[...] * v + rows.reshape(2, 8, 128)
        late()
        for s, h in LINKS[4:]:
            t_copy(par, s, h).wait_send()
            v_copy(par, s, h).wait_send()

        @inside
        def _():
            for s, h in LINKS[:4]:
                t_copy(par, s, h).wait_send()
                v_copy(par, s, h).wait_send()

        result = result + trecv[par, 1, g]
        for h in near:
            k = lax.rem(g + h, n_grp)
            for s in (OWN, IN):
                if s != OWN or h is not near[0]:
                    t_from(par, s, lax.rem(n_grp - h, n_grp)).wait_recv()
                    result = result + trecv[par, 1 - s * away, k]

        @inside
        def _():
            for h in near:
                t_from(par, OUT, lax.rem(n_grp - h, n_grp)).wait_recv()

        for h in near:
            result = result + trecv[par, 1 - away, lax.rem(g + h, n_grp)]
        return result

    me_a = (y * 4 + g) * 2 + core

    def a_copy(par, n):
        dy, dx = group_a[n]
        return pltpu.make_async_remote_copy(
            ra.at[par, me_a], ra.at[par, me_a], as_sem.at[n], ar_sem.at[par, me_a],
            device_id=peer_a(dy, dx, 1), device_id_type=MESH)

    def a_from(par, n, c):
        dy, dx = group_a[n]
        src = (lax.rem(y + 4 - dy, 4) * 4 + lax.rem(g + 4 - dx, 4)) * 2 + c
        return pltpu.make_async_remote_copy(
            ra.at[par, me_a], ra.at[par, src], as_sem.at[n], ar_sem.at[par, src],
            device_id=peer_a(dy, dx, 1), device_id_type=MESH)

    def b_copy(par, dz, c):
        return pltpu.make_async_remote_copy(
            rb.at[par, z], rb.at[par, z], bs_sem.at[c, dz], br_sem.at[par, z],
            device_id=peer_b(dz, c), device_id_type=MESH)

    def b_from(par, dz):
        src = lax.rem(z + zs - dz, zs)
        return pltpu.make_async_remote_copy(
            rb.at[par, z], rb.at[par, src], bs_sem.at[0, dz], br_sem.at[par, src],
            device_id=peer_b(dz, 1 - core), device_id_type=MESH)

    T0, T1, T2, G0, G1, G2, G3, X = range(8)

    def sum_start(par):
        basis = [st[T0], st[G0], st[T1], st[G1], st[T2] + st[G2]]
        items = [basis[i] * basis[j] for i in range(5) for j in range(i, 5)] + [dg[...]]
        both = jnp.concatenate([(a[0] + a[1])[None] for a in items], axis=0)
        flat = jnp.sum(jnp.sum(both, axis=1), axis=1, keepdims=True)
        keep = lax.broadcasted_iota(jnp.int32, (16, 128), 0) == lax.broadcasted_iota(
            jnp.int32, (16, 128), 1)
        row = jnp.sum(jnp.where(keep, jnp.broadcast_to(flat, (16, 128)), 0.0), axis=0, keepdims=True)
        ra[par, me_a] = row
        for n in A_ORDER:
            a_copy(par, n).start()

        @pl.when(core == 0)
        def _():
            a_copy(par, 0).start()

    def sum_middle(par):
        @pl.when(core == 1)
        def _():
            for n in range(16):
                a_from(par, n, 0).wait_recv()
                if n:
                    a_from(par, n, 1).wait_recv()
            rb[par, z] = jnp.sum(ra[par], axis=0)
            for n in b_order:
                b_copy(par, n, 0).start()
                b_copy(par, n, 1).start()
            b_copy(par, 0, 0).start()

        for n in range(1, 16):
            a_copy(par, n).wait_send()

        @pl.when(core == 0)
        def _():
            a_copy(par, 0).wait_send()

    def sum_end(par):
        for n in range(1, zs):
            b_from(par, n).wait_recv()

        @pl.when(core == 0)
        def _():
            b_from(par, 0).wait_recv()

        total = jnp.sum(rb[par], axis=0)

        @pl.when(core == 1)
        def _():
            for n in range(1, zs):
                b_copy(par, n, 0).wait_send()
                b_copy(par, n, 1).wait_send()
            b_copy(par, 0, 0).wait_send()

        return [jnp.broadcast_to(total[:, n : n + 1], (8, 128)) for n in range(16)]

    def two_steps(total):
        shift = cs[...]
        gram = {}
        n = 0
        for i in range(5):
            for j in range(i, 5):
                gram[i, j] = gram[j, i] = total[n]
                n += 1

        def form(a, b):
            whole = None
            for i, left in a.items():
                inner = None
                for j, right in b.items():
                    term = gram[i, j] * right
                    inner = term if inner is None else inner + term
                inner = left * inner
                whole = inner if whole is None else whole + inner
            return whole

        rr0 = gram[0, 0]
        pp = gram[0, 0] + 2.0 * gram[0, 1] + gram[1, 1]
        pbp = gram[0, 2] + gram[0, 3] + gram[1, 2] + gram[1, 3]
        al0 = rr0 / (shift * pp + pbp)
        b, e = -(al0 * shift), -al0
        a = 1.0 + b
        r1 = {0: a, 1: b, 2: e, 3: e}
        rr1 = form(r1, r1)
        be0 = rr1 / rr0
        pa, pb = a + be0, b + be0
        p1 = {0: pa, 1: pb, 2: e, 3: e}
        bp1 = {2: pa, 3: pb, 4: e}
        al1 = rr1 / (shift * form(p1, p1) + form(p1, bp1))
        sc = al1 * shift
        tail = e * (1.0 - sc)
        r2 = {0: a - sc * pa, 1: b - sc * pb, 2: tail - al1 * pa, 3: tail - al1 * pb, 4: -(al1 * e)}
        be1 = form(r2, r2) / rr1
        x0, x1 = al0 + al1 * pa, al0 + al1 * pb
        return r2, (be1 * pa, be1 * pb, be1 * e), (x0, x1, al1 * e)

    def advance(total, first):
        c, gg, xx = two_steps(total)
        t = [st[T0], st[T1], st[T2], first]
        q = [st[G0], st[G1], st[G2], st[G3]]
        h = [None, t[1] + q[1], t[2] + q[2], t[3] + q[3]]
        st[X] = st[X] + xx[0] * t[0] + xx[1] * q[0] + xx[2] * h[1]
        for k, n in enumerate((T0, T1, T2)):
            new = c[2] * t[k + 1] + c[3] * q[k + 1] + c[0] * t[k] + c[1] * q[k]
            st[n] = new if n == T2 else new + c[4] * h[k + 2]
        for k, n in enumerate((G0, G1, G2, G3)):
            new = gg[0] * t[k] + gg[1] * q[k]
            st[n] = new if n == G3 else new + gg[2] * h[k + 1]
        cf[0] = c[4]
        cf[1] = gg[2]

    r0 = deliver_end(1)
    st[T0] = r0
    st[T2] = r0

    def outer(o, carry):
        par = lax.rem(o, 2)

        def middle():
            @pl.when((o == 0) & (core == 1) & (z < zs - 1))
            def _():
                pl.semaphore_wait(ready, 2 * (zs - 1 - z))

            sum_middle(par)

        first = operate(0, st[T2], lambda: sum_start(par), lambda: None, False)

        def close_sum():
            total = sum_end(par)

            @pl.when(o == 0)
            def _():
                cs[...] = total[15] * (1.0 / (60.0 * faces_all)) + SHIFT

            @pl.when(o > 0)
            def _():
                advance(total, first)

        second = operate(1, first + st[G3], middle, close_sum, True)

        @pl.when(o == 0)
        def _():
            move = cs[...] - SHIFT
            inside = lax.broadcasted_iota(jnp.int32, (2, 8, 128), 0) * 8 + lax.broadcasted_iota(
                jnp.int32, (2, 8, 128), 1) < 15
            dg[...] = jnp.where(inside, dg[...] - move[None], 0.0)
            t1 = first - move * st[T0]
            st[T1] = t1
            st[T2] = second - move * (first + t1)

        @pl.when(o > 0)
        def _():
            st[T2] = st[T2] + cf[0] * second
            st[G3] = st[G3] + cf[1] * second

        return carry

    lax.fori_loop(0, 4, outer, 0)
    sum_start(0)
    sum_middle(0)
    r2, gg, xx = two_steps(sum_end(0))
    t, q = [st[T0], st[T1], st[T2]], [st[G0], st[G1], st[G2]]
    x = st[X] + xx[0] * t[0] + xx[1] * q[0] + xx[2] * (t[1] + q[1])
    r = (r2[4] * (t[2] + q[2]) + r2[2] * t[1] + r2[3] * q[1] + r2[0] * t[0] + r2[1] * q[0])
    sol_ref[...] = x.reshape(16, 128)[0:15]
    res_ref[...] = r.reshape(16, 128)[0:15]


def solution(mesh):
    n_dom, n_grp = mesh.shape["dom"], mesh.shape["grp"]

    def on_device(element_faces, interior_load, inverses, lift_operator, face_area, columns, blocks, diagonal):
        args = (element_faces, interior_load, inverses, lift_operator, face_area, columns, blocks, diagonal)
        slots, zs = columns.shape[0], n_dom // 8
        dma, vmem = pltpu.SemaphoreType.DMA, pltpu.VMEM
        faces_all = float(diagonal.shape[1] * n_dom)

        def body(*refs):
            kernel(n_dom, n_grp, faces_all, *refs)

        found = pl.pallas_call(
            body,
            out_shape=(jax.ShapeDtypeStruct(diagonal.shape, F32),) * 2,
            in_specs=[pl.BlockSpec(memory_space=pl.ANY)] * 8,
            out_specs=(pl.BlockSpec(memory_space=pltpu.VMEM),) * 2,
            scratch_shapes=[vmem(a.shape, a.dtype) for a in args]
            + [
                vmem((slots, n_grp, 15, 2, 8, 128), F32),
                vmem((2, 8, 128), F32),
                vmem((slots - 1, 8, 128), jnp.int32),
                vmem((slots - 1, 8, 128), jnp.int32),
                vmem((slots - 1, 3, 8, 128), jnp.int32),
                vmem((60, 384), F32),
                vmem((2, 3, 4, 2, 8, 128), F32),
                vmem((3, 4, 2, 8, 128), F32),
                vmem((2, 3, 4, 2, 8, 128), F32),
                vmem((slots, n_grp, 2, 8, 128), F32),
                vmem((2, 32, 1, 128), F32),
                vmem((2, zs, 1, 128), F32),
                vmem((8, 2, 8, 128), F32),
                vmem((8, 128), F32),
                vmem((2, 8, 128), F32),
                dma((8,)), dma((3, 4)), dma((2, 3, 4)), dma((3, 4)), dma((2, 3, 4)),
                dma((16,)), dma((2, 32)), dma((2, zs)), dma((2, zs)),
                pltpu.SemaphoreType.REGULAR,
            ],
            compiler_params=pltpu.CompilerParams(
                collective_id=0, has_side_effects=True, vmem_limit_bytes=40 * 1024 * 1024),
            name="cg",
        )(*[pltpu.with_memory_space_constraint(a, pltpu.HBM) for a in args])

        return found

    return jax.shard_map(
        on_device,
        mesh=mesh,
        in_specs=(
            P(None, "dom"), P(None, "dom"), P("grp", None, "dom"), P("grp", None), P(None, "dom"),
            P(None, "dom"), P(None, "grp", None, "dom"), P("grp", "dom"),
        ),
        out_specs=(P("grp", "dom"), P("grp", "dom")),
        check_vma=False,
    )
```
